128 devices in a mesh: blk: 16 (over z, x_lo, core), expert: 8 (over x_hi, y).
Axes of the slice: x: 4 (x_hi: 2, x_lo: 2; x = x_hi * 2 + x_lo), y: 4, z: 4, core: 2. Of those that a mesh axis runs over, the one named last changes fastest.
Arguments:
- new_tokens: bfloat16 [8, 2048, 2048], P('expert', 'blk'), may hold values from -6 to 6
- norm_gain: float32 [2048], replicated, may hold values from 0.5 to 1.5
- router_weight: bfloat16 [2048, 8], replicated, may hold values from -0.125 to 0.125
- att_choice: int32 [8, 2048, 2], P('expert', 'blk'), may hold values from 0 to 7, all different within a row; in each aligned block of 128 rows (0 to 127, 128 to 255, ..., all dimensions but the last counted through in order) at most 64 rows name the same one
- w_query: bfloat16 [8, 2048, 1024], P('expert'), may hold values from -0.125 to 0.125
- w_key: bfloat16 [2048, 1024], replicated, may hold values from -0.375 to 0.375
- w_value: bfloat16 [2048, 1024], replicated, may hold values from -0.125 to 0.125
- w_out: bfloat16 [8, 1024, 2048], P('expert'), may hold values from -0.1875 to 0.1875
- cache_keys: bfloat16 [8, 5120, 1024], P('expert', 'blk'), may hold values from -12 to 12
- cache_values: bfloat16 [8, 5120, 1024], P('expert', 'blk'), may hold values from -6 to 6
- hidden_held: bfloat16 [8, 512, 2048], P('expert', 'blk'), may hold values from -6 to 6
- recompute_ids: int32 [8, 16], P('expert', 'blk'), may hold values from 0 to 9
- block_live: int32 [8, 160], P('expert', 'blk'), may hold values 0 or 1
- cached_len: int32 [8], P('expert'), may hold values from 1 to 5120, as said below
Outputs:
- layer_out: bfloat16 [8, 2048, 2048], P('expert', 'blk')
The draws below stay inside these ranges and needn't reach their ends.
Inputs may be any that keep to these rules, and one draw needn't show every extreme that they name: `att_choice`: a token's two choices differ; among the tokens of one index of blk and expert, at most 64 name any one expert. `cached_len`: one request in every draw has exactly 5120 cached tokens.
All inputs are finite; a program needn't handle non-finite values. No bound on the sum of `block_live` on one device may be relied on, other than what follows from the above.
Results may differ from the reference program's by a relative error of at most 0.012.
Values may be sent and summed in bfloat16 or wider, within the bound.
A program may use at most 192 MiB of HBM per device.

```python
import math
import jax
import jax.numpy as jnp
import numpy as np
from jax import lax

D = 2048
HD = 128
KVH = 8
KVW = 1024
ATT_EXPERTS = 8
REQS = 8
NEW_DEV = 128
NEW = 2048
CACHE_DEV = 320
CB = 32
BLK_DEV = 10
BLOCKS = 160
L_MAX = 5120
CAP = 64
HELD = 512
N_BLK = 16


def draw_cached_len(key, part):
    first_key, second_key = jax.random.split(key)
    lengths = jax.random.randint(first_key, (REQS,), 1, L_MAX + 1)
    longest = jax.random.randint(second_key, (), 0, REQS)
    return jnp.where(jnp.arange(REQS) == longest, L_MAX, lengths).astype(jnp.int32)


def with_ends(drawn, stream_key, smallest, top_value):
    longest = drawn.shape.index(max(drawn.shape))
    spots = []
    for shift in (0, 1):
        where = [jax.random.randint(jax.random.fold_in(stream_key, axis), (), 0, length) for axis, length in enumerate(drawn.shape)]
        where[longest] = (where[longest] + shift) % drawn.shape[longest]
        spots.append(tuple(where))
    return drawn.at[spots[0]].set(smallest).at[spots[1]].set(top_value)


def levels(stream_key, dims, cuts, low, largest):
    def one(axis_at, parts):
        steps = jax.random.uniform(jax.random.fold_in(jax.random.fold_in(stream_key, 6), axis_at), (parts,), jnp.float32, low / len(cuts), largest / len(cuts))
        return jnp.repeat(jnp.exp(steps), dims[axis_at] // parts).reshape((-1,) + (1,) * (len(dims) - axis_at - 1))

    level = one(*cuts[0])
    for cut in cuts[1:]:
        level = level * one(*cut)
    return level


def assign_block(rng, own, number, rows, number_of, top, reach, lean):
    order = jax.random.permutation(rng, number_of)
    packed, common = load_shares(number_of, rows * top, reach, lean, True), load_shares(number_of, rows * top, reach, lean, False)
    places = jnp.arange(number_of)

    def named(sizes, rotation):
        used = int((sizes > 0).sum())
        fixed = max(1, used // 4)
        shifted = fixed + (places - fixed + rotation * (used - fixed)) % max(1, number_of - fixed)
        return jnp.zeros((number_of,), jnp.int32).at[order[jnp.where(places < fixed, places, shifted)]].set(jnp.asarray(sizes, jnp.int32))

    sizes = jnp.where(number % 4 == 0, named(packed, number // 4), named(common, number - number // 4 - 1))
    mixed = jax.random.permutation(jax.random.fold_in(own, 3), number_of)
    giver, sink = mixed[0:number_of // 2 * 2:2], mixed[1:number_of // 2 * 2:2]
    slack = jnp.minimum(sizes[giver] - 1, reach - sizes[sink]) // 2
    slack = jnp.where((giver == order[0]) | (sink == order[0]) | (sizes[sink] == 0), 0, jnp.maximum(slack, 0))
    shifted = jax.random.randint(jax.random.fold_in(own, 4), (number_of // 2,), 0, 1 << 20) % (slack + 1)
    sizes = sizes.at[giver].add(-shifted).at[sink].add(shifted)
    members = jnp.searchsorted(jnp.cumsum(sizes), jnp.arange(rows * top), side="right").astype(jnp.int32)
    table = members.reshape(top, rows).T
    table = table[jax.random.permutation(jax.random.fold_in(own, 1), rows)]
    rotation = jax.random.randint(jax.random.fold_in(own, 2), (rows, 1), 0, top)
    return jnp.take_along_axis(table, (jnp.arange(top)[None, :] + rotation) % top, axis=1)


def load_shares(amount, total, reach, lean, full):
    portions = [(1 << 20) // math.isqrt(grade ** lean) + 1 for grade in range(1, amount + 1)]
    largest = reach if full else min(reach, max(-(-total // amount), total * portions[0] // sum(portions)))
    least = 1 if total - largest >= amount - 1 else 0
    holding, spare = [largest] + [least] * (amount - 1), total - largest - least * (amount - 1)
    while spare > 0:
        movable = [i for i in range(1, amount) if holding[i] < largest] or [i for i in range(1, amount) if holding[i] < reach]
        mass, remaining = sum([portions[i] for i in movable]), spare
        for i in movable:
            more = min(reach - holding[i], max(1, remaining * portions[i] // mass), spare)
            holding[i] = holding[i] + more
            spare = spare - more
    return np.array(holding)


def scatter_about(key, dims, spread, reach, pieces=(), kind=jnp.bfloat16):
    entries = jax.random.normal(key, dims, jnp.float32) * spread
    if len(pieces) > 0:
        entries = levels(key, dims, pieces, -0.22, 0.18) * entries
    return jnp.clip(entries, min=-reach, max=reach).astype(kind)


def setup_inputs(seed: int = 0) -> dict:
    streams_of = jax.random.split(jax.random.key(seed), 15)
    new_tokens = scatter_about(streams_of[0], (REQS, NEW, D), 1.0, 6.0, ((0, 8), (1, 16)))
    norm_gain = jnp.clip(1.0 + 0.1 * jax.random.normal(streams_of[1], (D,), jnp.float32), 0.5, 1.5)
    router_weight = scatter_about(streams_of[2], (D, ATT_EXPERTS), D ** -0.5, 0.125)
    att_choice_keys = jax.random.split(jax.random.fold_in(streams_of[3], 1), REQS * NEW // NEW_DEV)
    att_choice_turns = jax.random.permutation(jax.random.fold_in(streams_of[3], 3), REQS * NEW // NEW_DEV)
    att_choice = jax.vmap(lambda own, number: assign_block(jax.random.fold_in(streams_of[3], 2), own, number, NEW_DEV, ATT_EXPERTS, 2, CAP, 2))(att_choice_keys, att_choice_turns).reshape((REQS, NEW, 2))
    w_query = scatter_about(streams_of[4], (ATT_EXPERTS, D, KVW), D ** -0.5, 0.125, ((0, 8),))
    w_key = scatter_about(streams_of[5], (D, KVW), (D // 9) ** -0.5, 0.375)
    w_value = scatter_about(streams_of[6], (D, KVW), D ** -0.5, 0.125)
    w_out = scatter_about(streams_of[7], (ATT_EXPERTS, KVW, D), KVW ** -0.5, 0.1875, ((0, 8),))
    cache_keys = scatter_about(streams_of[8], (REQS, L_MAX, KVW), 3.0, 12.0, ((0, 8), (1, 16)))
    cache_values = scatter_about(streams_of[9], (REQS, L_MAX, KVW), 1.0, 6.0, ((0, 8), (1, 16)))
    hidden_held = scatter_about(streams_of[10], (REQS, HELD, D), 1.0, 6.0, ((0, 8), (1, 16)))
    recompute_ids = with_ends(jax.random.randint(streams_of[11], (REQS, N_BLK), 0, BLK_DEV), jax.random.fold_in(streams_of[11], 1), 0, BLK_DEV - 1).astype(jnp.int32)
    block_live = with_ends((jax.random.randint(streams_of[12], (REQS, BLOCKS), 0, 8) < 7).astype(jnp.int32), jax.random.fold_in(streams_of[12], 1), 0, 1)
    cached_len = draw_cached_len(jax.random.fold_in(streams_of[14], 71), 0)
    return {"new_tokens": new_tokens, "norm_gain": norm_gain, "router_weight": router_weight, "att_choice": att_choice, "w_query": w_query, "w_key": w_key, "w_value": w_value, "w_out": w_out, "cache_keys": cache_keys, "cache_values": cache_values, "hidden_held": hidden_held, "recompute_ids": recompute_ids, "block_live": block_live, "cached_len": cached_len}


epsilon = 1e-06
theta_base = 10000.0
far_position = 1073741824

def rounded(values):
    return lax.optimization_barrier(values.astype(jnp.bfloat16))

def normalize(hidden, norm_gain):
    widened = hidden.astype(jnp.float32)
    inverse = lax.rsqrt(lax.optimization_barrier(jnp.mean(widened * widened, axis=-1, keepdims=True)) + epsilon)
    return rounded(widened * inverse * norm_gain)

def rotate(projected, positions):
    row_count = projected.shape[0]
    half_width = HD // 2
    separated = projected.reshape(row_count, KVH, HD)
    frequency = jnp.exp(jnp.arange(half_width, dtype=jnp.float32) * (-math.log(theta_base) / half_width))
    angles = positions.astype(jnp.float32)[:, None] * frequency[None, :]
    cosine = jnp.cos(angles)[:, None, :]
    sine_part = jnp.sin(angles)[:, None, :]
    first_half = separated[..., :half_width]
    second_half = separated[..., half_width:]
    turned = jnp.concatenate([first_half * cosine - second_half * sine_part, second_half * cosine + first_half * sine_part], axis=-1)
    return turned.reshape(row_count, KVH * HD)

def attend(queries, query_pos, key_rows, value_rows, key_pos):
    score_scale = 1.0 / math.sqrt(HD)
    key_heads = key_rows.reshape(key_rows.shape[0], KVH, HD).astype(jnp.float32)
    value_heads = value_rows.reshape(value_rows.shape[0], KVH, HD).astype(jnp.float32)
    scores = jnp.einsum('qhd,khd->qhk', queries.astype(jnp.float32), key_heads) * score_scale
    allowed = key_pos[None, None, :] <= query_pos[:, None, None]
    weights = rounded(jnp.where(allowed, jnp.exp(scores), 0.0)).astype(jnp.float32)
    denominator = lax.optimization_barrier(jnp.sum(weights, axis=-1))
    numerator = jnp.einsum('qhk,khd->qhd', weights, value_heads)
    return (numerator, denominator)

def reference(new_tokens, norm_gain, router_weight, att_choice, w_query, w_key, w_value, w_out, cache_keys, cache_values, hidden_held, recompute_ids, block_live, cached_len):
    experts = w_query.shape[0]
    all_rows = 2 * NEW
    block_rows = math.gcd(512, all_rows)
    query_weight = w_query.astype(jnp.float32)
    results = []
    for request in range(REQS):
        length = cached_len[request]
        tokens = new_tokens[request]
        normed = normalize(tokens, norm_gain)
        new_pos = length + jnp.arange(NEW, dtype=jnp.int32)
        logits = jnp.dot(normed, router_weight, preferred_element_type=jnp.float32)
        picked = att_choice[request]
        chosen = jnp.take_along_axis(logits, picked, axis=1)
        gate_first = jax.nn.sigmoid(chosen[:, 0] - chosen[:, 1])
        new_keys = rounded(rotate(jnp.dot(normed, w_key, preferred_element_type=jnp.float32), new_pos))
        new_values = rounded(jnp.dot(normed, w_value, preferred_element_type=jnp.float32))
        held_norm = normalize(hidden_held[request], norm_gain)
        held_pos = (jnp.arange(N_BLK, dtype=jnp.int32)[:, None] * CACHE_DEV + recompute_ids[request][:, None] * CB + jnp.arange(CB, dtype=jnp.int32)[None, :]).reshape(-1)
        held_keys = rounded(rotate(jnp.dot(held_norm, w_key, preferred_element_type=jnp.float32), held_pos))
        held_values = rounded(jnp.dot(held_norm, w_value, preferred_element_type=jnp.float32))
        key_rows = jnp.concatenate([cache_keys[request].at[held_pos].set(held_keys), new_keys], axis=0)
        value_rows = jnp.concatenate([cache_values[request].at[held_pos].set(held_values), new_values], axis=0)
        cache_pos = jnp.arange(L_MAX, dtype=jnp.int32)
        usable = (cache_pos < length) & (block_live[request][cache_pos // CB] == 1)
        key_pos = jnp.concatenate([jnp.where(usable, cache_pos, far_position), new_pos])
        projections = jnp.einsum('td,edk->etk', normed.astype(jnp.float32), query_weight)
        selected = projections[picked, jnp.arange(NEW)[:, None]].reshape(all_rows, KVH * HD)
        query_rows = rounded(rotate(selected, jnp.repeat(new_pos, 2)))
        query_pos = length + jnp.arange(all_rows, dtype=jnp.int32) // 2
        query_blocks = query_rows.reshape(all_rows // block_rows, block_rows, KVH, HD)
        position_blocks = query_pos.reshape(all_rows // block_rows, block_rows)

        def one_block(block_pair):
            return attend(block_pair[0], block_pair[1], key_rows, value_rows, key_pos)
        numerator, denominator = lax.map(one_block, (query_blocks, position_blocks))
        numerator = numerator.reshape(all_rows, KVH, HD)
        denominator = denominator.reshape(all_rows, KVH)
        attended = rounded((numerator / denominator[..., None]).reshape(all_rows, KVH * HD)).astype(jnp.float32)
        expert_of_row = picked.reshape(-1)
        expert_out = jnp.zeros((all_rows, D), jnp.float32)
        for expert in range(experts):
            projected = rounded(jnp.dot(attended, w_out[expert].astype(jnp.float32))).astype(jnp.float32)
            expert_out = jnp.where((expert_of_row == expert)[:, None], projected, expert_out)
        combined = tokens.astype(jnp.float32) + gate_first[:, None] * expert_out[0::2] + (1.0 - gate_first)[:, None] * expert_out[1::2]
        results.append(combined.astype(jnp.bfloat16))
    return jnp.stack(results)
```

```python
import functools
import math

import jax
import jax.numpy as jnp
from jax import lax
from jax.experimental import pallas as pl
from jax.experimental.pallas import tpu as pltpu
from jax.sharding import PartitionSpec as P

HD = 128
KVH = 8
CB = 32
CAP = 64
D = 2048
KVW = KVH * HD
NEW_DEV = 128
CACHE_DEV = 320
KEYS = NEW_DEV + CACHE_DEV
HALF = KEYS // 2
EXPERTS = 8
SLOTS = EXPERTS * CAP
ROWS = 2 * NEW_DEV
KC = 4
KW = D // KC
NC = 4
NW = D // NC
NZ = 4

epsilon = 1e-06
theta_base = 10000.0
MASKED = -1e30
LOG2E = 1.4426950408889634
SCALE = LOG2E / math.sqrt(HD)


def normalize(hidden, norm_gain):
    widened = hidden.astype(jnp.float32)
    inverse = lax.rsqrt(jnp.mean(widened * widened, axis=-1, keepdims=True) + epsilon)
    return (widened * inverse * norm_gain).astype(jnp.bfloat16)


def rope_tables(positions):
    half_width = HD // 2
    frequency = jnp.exp(
        jnp.arange(half_width, dtype=jnp.float32) * (-math.log(theta_base) / half_width)
    )
    angles = positions.astype(jnp.float32)[:, None] * frequency[None, :]
    cosine = jnp.cos(angles)
    sine = jnp.sin(angles)
    return jnp.concatenate([cosine, cosine], 1), jnp.concatenate([-sine, sine], 1)


def rotate(projected, cosine, sine):
    row_count = projected.shape[0]
    half_width = HD // 2
    v = projected.reshape(row_count, KVH, HD)
    swapped = jnp.concatenate([v[..., half_width:], v[..., :half_width]], axis=-1)
    return v * cosine[:, None, :] + swapped * sine[:, None, :]


def kernel(
    kv_own,
    bias_own,
    rows_send,
    gather_q,
    spread_q,
    gates,
    cosine,
    sine,
    tokens,
    w_query,
    w_out,
    out,
    kv,
    bias,
    rows,
    wq,
    wo,
    qacc,
    qsend,
    qret,
    queries,
    acc,
    own_part,
    num_send,
    num_recv,
    den_send,
    den_recv,
    att_send,
    att_recv,
    exp_send,
    exp_recv,
    local_sem,
    rows_s,
    rows_r,
    qs_s,
    qs_r,
    kv_s,
    kv_r,
    bias_s,
    bias_r,
    qx_s,
    qx_r,
    num_s,
    num_r,
    den_s,
    den_r,
    att_s,
    att_r,
    exp_s,
    exp_r,
):
    blk = lax.axis_index("blk")
    expert = lax.axis_index("expert")
    z = blk // 4
    xl = (blk // 2) % 2
    c = blk % 2
    xh = expert // 4
    y = expert % 4

    def at_blk(zz, xx, cc):
        return {"blk": zz * 4 + xx * 2 + cc, "expert": expert}

    def peer(off):
        return ((xh + off // 4) % 2) * 4 + (y + off % 4) % 4

    def at_expert(e):
        return {"blk": blk, "expert": e}

    zp = (z + 1) % NZ
    zm = (z + NZ - 1) % NZ
    zo = (z + 2) % NZ
    up = at_blk(zp, xl, c)
    down = at_blk(zm, xl, c)
    partner = at_blk(z, xl, 1 - c)
    across = at_blk(z, 1 - xl, c)
    mine = z * 2 + c

    def remote(src, dst, ssem, rsem, device):
        return pltpu.make_async_remote_copy(
            src_ref=src,
            dst_ref=dst,
            send_sem=ssem,
            recv_sem=rsem,
            device_id=device,
            device_id_type=pl.DeviceIdType.MESH,
        )

    barrier = pltpu.get_barrier_semaphore()
    for off in range(1, 8):
        pl.semaphore_signal(
            barrier, inc=1, device_id=at_expert(peer(off)), device_id_type=pl.DeviceIdType.MESH
        )
        pl.semaphore_signal(
            barrier,
            inc=1,
            device_id=at_blk((z + off // 2) % NZ, xl, (c + off % 2) % 2),
            device_id_type=pl.DeviceIdType.MESH,
        )
    pl.semaphore_signal(barrier, inc=1, device_id=across, device_id_type=pl.DeviceIdType.MESH)

    load_wq = pltpu.make_async_copy(w_query, wq, local_sem.at[0])
    load_wo = pltpu.make_async_copy(w_out, wo, local_sem.at[1])
    load_kv = pltpu.make_async_copy(kv_own, kv.at[:, mine], local_sem.at[2])
    load_wq.start()
    load_kv.start()
    load_wo.start()
    pl.semaphore_wait(barrier, 15)

    def rows_copy(k, off):
        e = peer(off)
        return remote(
            rows_send.at[e, :, pl.ds(pl.multiple_of(k * KW, KW), KW)],
            rows.at[k, expert],
            rows_s.at[k, off],
            rows_r.at[k, off],
            at_expert(e),
        )

    def rows_local(k):
        return pltpu.make_async_copy(
            rows_send.at[expert, :, pl.ds(pl.multiple_of(k * KW, KW), KW)],
            rows.at[k, expert],
            local_sem.at[3 + k],
        )

    def kv_own_copy(h, way):
        return remote(
            kv_own.at[h],
            kv.at[h, mine],
            kv_s.at[h, way],
            kv_r.at[h, way],
            (up, down, partner)[way],
        )

    def kv_forward(h, way):
        source = (zm, zp)[way] * 2 + c
        part = pl.ds(way * HALF, HALF)
        return remote(
            kv.at[h, source, part],
            kv.at[h, source, part],
            kv_s.at[h, 3 + way],
            kv_r.at[h, 3 + way],
            (up, down)[way],
        )

    def kv_share(h, which):
        if which < 2:
            ref = kv.at[h, (zm, zp)[which] * 2 + c]
        else:
            ref = kv.at[h, zo * 2 + c, pl.ds((which - 2) * HALF, HALF)]
        return remote(ref, ref, kv_s.at[h, 5 + which], kv_r.at[h, 5 + which], partner)

    def bias_copy(off):
        return remote(
            bias_own,
            bias.at[mine],
            bias_s.at[off],
            bias_r.at[off],
            at_blk((z + off // 2) % NZ, xl, (c + off % 2) % 2),
        )

    def send_rows(k, _):
        for off in range(1, 8):
            rows_copy(k, off).start()
        rows_local(k).start()
        return 0

    lax.fori_loop(0, KC, send_rows, 0)

    def send_kv(h, _):
        for way in range(3):
            kv_own_copy(h, way).start()
        return 0

    lax.fori_loop(0, KVH, send_kv, 0)
    for off in range(1, 8):
        bias_copy(off).start()
    bias[mine] = bias_own[...]

    load_wq.wait()

    def project(k, _):
        for off in range(1, 8):
            rows_copy(k, off).wait_recv()
        rows_local(k).wait()
        part = jnp.dot(
            rows[k].reshape(SLOTS, KW),
            wq[pl.ds(pl.multiple_of(k * KW, KW), KW), :],
            preferred_element_type=jnp.float32,
        )

        @pl.when(k == 0)
        def _():
            qacc[...] = part

        @pl.when(k > 0)
        def _():
            qacc[...] += part

        return 0

    lax.fori_loop(0, KC, project, 0)
    qsend[...] = qacc[...].astype(jnp.bfloat16).reshape(EXPERTS, CAP, KVW)

    def q_copy(off):
        r = peer(off)
        return remote(
            qsend.at[r], qret.at[expert], qs_s.at[off], qs_r.at[off], at_expert(r)
        )

    for off in range(1, 8):
        q_copy(off).start()
    q_local = pltpu.make_async_copy(qsend.at[expert], qret.at[expert], local_sem.at[7])
    q_local.start()

    def pass_on(h, _):
        for way in range(2):
            kv_own_copy(h, way).wait_recv()
            kv_forward(h, way).start()
        for way in range(2):
            kv_share(h, way).start()
        return 0

    lax.fori_loop(0, KVH, pass_on, 0)

    for off in range(1, 8):
        q_copy(off).wait_recv()
    q_local.wait()
    gathered = jnp.dot(
        gather_q[...], qret[...].reshape(SLOTS, KVW), preferred_element_type=jnp.float32
    )
    for h in range(KVH):
        v = gathered[:, h * HD : (h + 1) * HD]
        turned = v * cosine[...] + pltpu.roll(v, HD // 2, 1) * sine[...]
        queries[h, 0:ROWS] = turned.astype(jnp.bfloat16)

    def qx_copy(h):
        return remote(
            queries.at[h, pl.ds(0, ROWS)],
            queries.at[h, pl.ds(ROWS, ROWS)],
            qx_s.at[h],
            qx_r.at[h],
            across,
        )

    for h in range(KVH):
        qx_copy(h).start()
    for off in range(1, 8):
        bias_copy(off).wait_recv()
    load_kv.wait()

    lead = (
        lax.broadcasted_iota(jnp.int32, (ROWS, NEW_DEV), 0) % NEW_DEV
        - lax.broadcasted_iota(jnp.int32, (ROWS, NEW_DEV), 1)
    )

    def block(h, zz, cc):
        j = zz * 2 + cc
        keys = kv[h, j, :, 0:HD]
        values = kv[h, j, :, HD : 2 * HD]
        scores = lax.dot_general(
            queries[h], keys, (((1,), (1,)), ((), ())), preferred_element_type=jnp.float32
        )
        offset_own = jnp.clip((j - mine) * NEW_DEV, -NEW_DEV, NEW_DEV)
        offset_across = jnp.clip(2 * (zz - z) + 2 * xl - 1, -1, 1) * NEW_DEV
        fresh = jnp.exp2(scores[:, 0:NEW_DEV] * SCALE)
        fresh = jnp.concatenate(
            [
                jnp.where(lead >= offset_own, fresh[0:ROWS], 0.0),
                jnp.where(lead >= offset_across, fresh[ROWS:], 0.0),
            ],
            axis=0,
        )
        old = jnp.exp2(scores[:, NEW_DEV:] * SCALE + bias[j, 0:1, 0:CACHE_DEV])
        weights = jnp.concatenate(
            [fresh.astype(jnp.bfloat16), old.astype(jnp.bfloat16)], axis=1
        )
        extended = jnp.concatenate([values, jnp.ones((KEYS, HD), jnp.bfloat16)], axis=1)
        acc[...] += jnp.dot(weights, extended, preferred_element_type=jnp.float32)

    def num_copy(h):
        return remote(num_send.at[h], num_recv.at[h], num_s.at[h], num_r.at[h], across)

    def den_copy(h):
        return remote(den_send.at[h], den_recv.at[h], den_s.at[h], den_r.at[h], across)

    def att_copy(h, off):
        e = peer(off)
        return remote(
            att_send.at[h, e],
            att_recv.at[h, expert],
            att_s.at[h, off],
            att_r.at[h, off],
            at_expert(e),
        )

    def att_local(h):
        return pltpu.make_async_copy(
            att_send.at[h, expert], att_recv.at[h, expert], local_sem.at[8 + h]
        )

    def finish(h):
        num_copy(h).wait_recv()
        den_copy(h).wait_recv()
        den_there = jnp.broadcast_to(den_recv[h][0:1, :], (HD, ROWS)).T
        numerator = own_part[h, :, 0:HD] + num_recv[h].astype(jnp.float32)
        denominator = own_part[h, :, HD:] + den_there
        attended = (numerator / denominator).astype(jnp.bfloat16)
        spread = jnp.dot(spread_q[...], attended, preferred_element_type=jnp.float32)
        att_send[h] = spread.astype(jnp.bfloat16).reshape(EXPERTS, CAP, HD)
        for off in range(1, 8):
            att_copy(h, off).start()
        att_local(h).start()

    def one_head(h, _):
        for way in range(2):
            kv_forward(h, way).wait_recv()
            kv_share(h, 2 + way).start()
        qx_copy(h).wait_recv()
        acc[...] = jnp.zeros_like(acc)

        def first(zz, _):
            block(h, zz, c)
            return 0

        lax.fori_loop(0, NZ, first, 0)
        kv_own_copy(h, 2).wait_recv()
        for which in range(4):
            kv_share(h, which).wait_recv()

        def second(zz, _):
            block(h, zz, 1 - c)
            return 0

        lax.fori_loop(0, NZ, second, 0)
        own_part[h] = acc[0:ROWS]
        num_send[h] = acc[ROWS:, 0:HD].astype(jnp.bfloat16)
        den_send[h] = acc[ROWS:, HD:].T[0:8, :]
        num_copy(h).start()
        den_copy(h).start()

        @pl.when(h >= 2)
        def _():
            finish(h - 2)

        return 0

    lax.fori_loop(0, KVH, one_head, 0)
    finish(KVH - 2)
    finish(KVH - 1)

    load_wo.wait()

    def wait_att(h, _):
        for off in range(1, 8):
            att_copy(h, off).wait_recv()
        att_local(h).wait()
        return 0

    lax.fori_loop(0, KVH, wait_att, 0)

    def exp_copy(n, off):
        r = peer(off)
        return remote(
            exp_send.at[n, r],
            exp_recv.at[n, expert],
            exp_s.at[n, off],
            exp_r.at[n, off],
            at_expert(r),
        )

    def exp_local(n):
        return pltpu.make_async_copy(
            exp_send.at[n, expert], exp_recv.at[n, expert], local_sem.at[16 + n]
        )

    arrived = jnp.concatenate([att_recv[h].reshape(SLOTS, HD) for h in range(KVH)], axis=1)

    def project_out(n, _):
        part = jnp.dot(
            arrived,
            wo[:, pl.ds(pl.multiple_of(n * NW, NW), NW)],
            preferred_element_type=jnp.float32,
        )
        exp_send[n] = part.astype(jnp.bfloat16).reshape(EXPERTS, CAP, NW)
        for off in range(1, 8):
            exp_copy(n, off).start()
        exp_local(n).start()
        return 0

    lax.fori_loop(0, NC, project_out, 0)

    def combine(n, _):
        for off in range(1, 8):
            exp_copy(n, off).wait_recv()
        exp_local(n).wait()
        back = exp_recv[n].reshape(SLOTS, NW)
        columns = pl.ds(pl.multiple_of(n * NW, NW), NW)
        mixed = jnp.dot(gates[:, 0:SLOTS], back, preferred_element_type=jnp.float32)
        mixed += jnp.dot(gates[:, SLOTS:], back, preferred_element_type=jnp.float32)
        out[:, columns] = (tokens[:, columns].astype(jnp.float32) + mixed).astype(jnp.bfloat16)
        return 0

    lax.fori_loop(0, NC, combine, 0)

    def drain_rows(k, _):
        for off in range(1, 8):
            rows_copy(k, off).wait_send()
            exp_copy(k, off).wait_send()
        return 0

    lax.fori_loop(0, KC, drain_rows, 0)

    def drain_heads(h, _):
        for way in range(3):
            kv_own_copy(h, way).wait_send()
        for way in range(2):
            kv_forward(h, way).wait_send()
        for which in range(4):
            kv_share(h, which).wait_send()
        qx_copy(h).wait_send()
        num_copy(h).wait_send()
        den_copy(h).wait_send()
        for off in range(1, 8):
            att_copy(h, off).wait_send()
        return 0

    lax.fori_loop(0, KVH, drain_heads, 0)
    for off in range(1, 8):
        bias_copy(off).wait_send()
        q_copy(off).wait_send()


def layer(kv_own, bias_own, rows_send, gather_q, spread_q, gates, cosine, sine, tokens, wq, wo):
    bf = jnp.bfloat16
    f32 = jnp.float32
    anywhere = pl.BlockSpec(memory_space=pl.ANY)
    inside = pl.BlockSpec(memory_space=pltpu.VMEM)
    dma = pltpu.SemaphoreType.DMA
    return pl.pallas_call(
        kernel,
        out_shape=jax.ShapeDtypeStruct((NEW_DEV, D), bf),
        in_specs=[anywhere, inside, anywhere] + [inside] * 6 + [anywhere] * 2,
        out_specs=inside,
        scratch_shapes=[
            pltpu.VMEM((KVH, 2 * NZ, KEYS, 2 * HD), bf),
            pltpu.VMEM((2 * NZ, 8, 384), f32),
            pltpu.VMEM((KC, EXPERTS, CAP, KW), bf),
            pltpu.VMEM((D, KVW), bf),
            pltpu.VMEM((KVW, D), bf),
            pltpu.VMEM((SLOTS, KVW), f32),
            pltpu.VMEM((EXPERTS, CAP, KVW), bf),
            pltpu.VMEM((EXPERTS, CAP, KVW), bf),
            pltpu.VMEM((KVH, 2 * ROWS, HD), bf),
            pltpu.VMEM((2 * ROWS, 2 * HD), f32),
            pltpu.VMEM((KVH, ROWS, 2 * HD), f32),
            pltpu.VMEM((KVH, ROWS, HD), bf),
            pltpu.VMEM((KVH, ROWS, HD), bf),
            pltpu.VMEM((KVH, 8, ROWS), f32),
            pltpu.VMEM((KVH, 8, ROWS), f32),
            pltpu.VMEM((KVH, EXPERTS, CAP, HD), bf),
            pltpu.VMEM((KVH, EXPERTS, CAP, HD), bf),
            pltpu.VMEM((NC, EXPERTS, CAP, NW), bf),
            pltpu.VMEM((NC, EXPERTS, CAP, NW), bf),
            dma((20,)),
            dma((KC, 8)),
            dma((KC, 8)),
            dma((8,)),
            dma((8,)),
            dma((KVH, 9)),
            dma((KVH, 9)),
            dma((8,)),
            dma((8,)),
            dma((KVH,)),
            dma((KVH,)),
            dma((KVH,)),
            dma((KVH,)),
            dma((KVH,)),
            dma((KVH,)),
            dma((KVH, 8)),
            dma((KVH, 8)),
            dma((NC, 8)),
            dma((NC, 8)),
        ],
        compiler_params=pltpu.CompilerParams(
            collective_id=0, has_side_effects=True, vmem_limit_bytes=60 * 1024 * 1024
        ),
        name="layer",
    )(kv_own, bias_own, rows_send, gather_q, spread_q, gates, cosine, sine, tokens, wq, wo)


def shards(
    new_tokens,
    norm_gain,
    router_weight,
    att_choice,
    w_query,
    w_key,
    w_value,
    w_out,
    cache_keys,
    cache_values,
    hidden_held,
    recompute_ids,
    block_live,
    cached_len,
):
    bf = jnp.bfloat16
    f32 = jnp.float32
    blk_index = lax.axis_index("blk")
    length = cached_len[0]
    tokens = new_tokens[0]
    normed = normalize(tokens, norm_gain)
    held_norm = normalize(hidden_held[0], norm_gain)
    new_pos = length + blk_index * NEW_DEV + jnp.arange(NEW_DEV, dtype=jnp.int32)
    held_start = recompute_ids[0, 0] * CB
    held_pos = blk_index * CACHE_DEV + held_start + jnp.arange(CB, dtype=jnp.int32)
    both_rows = jnp.concatenate([normed, held_norm], axis=0)
    cosine, sine = rope_tables(jnp.concatenate([new_pos, held_pos]))
    key_proj = rotate(
        jnp.dot(both_rows, w_key, preferred_element_type=f32), cosine, sine
    ).astype(bf)
    value_proj = (
        jnp.dot(both_rows, w_value, preferred_element_type=f32).astype(bf).reshape(-1, KVH, HD)
    )
    fresh = jnp.concatenate([key_proj, value_proj], axis=-1).transpose(1, 0, 2)
    cached = jnp.concatenate(
        [cache_keys[0].reshape(-1, KVH, HD), cache_values[0].reshape(-1, KVH, HD)], axis=-1
    ).transpose(1, 0, 2)
    kv_own = jnp.concatenate([fresh[:, :NEW_DEV], cached], axis=1)
    kv_own = lax.dynamic_update_slice(
        kv_own, fresh[:, NEW_DEV:], (0, NEW_DEV + held_start, 0)
    )
    slot_pos = blk_index * CACHE_DEV + jnp.arange(CACHE_DEV, dtype=jnp.int32)
    usable = (slot_pos < length) & (jnp.repeat(block_live[0], CB) == 1)
    bias_own = jnp.where(usable, 0.0, MASKED).astype(f32)
    bias_own = jnp.broadcast_to(jnp.pad(bias_own, (0, 384 - CACHE_DEV))[None], (8, 384))

    logits = jnp.dot(normed, router_weight, preferred_element_type=f32)
    picked = att_choice[0]
    ids = jnp.arange(EXPERTS, dtype=jnp.int32)
    one_hot = picked.T.reshape(-1)[:, None] == ids[None, :]
    chosen = jnp.sum(jnp.where(one_hot, jnp.concatenate([logits, logits], 0), 0.0), axis=1)
    gate_first = jax.nn.sigmoid(chosen[:NEW_DEV] - chosen[NEW_DEV:])
    order = jnp.arange(ROWS, dtype=jnp.int32)
    earlier = (order[:, None] > order[None, :]).astype(bf)
    before = jnp.dot(earlier, one_hot.astype(bf), preferred_element_type=f32)
    slot = jnp.sum(jnp.where(one_hot, before, 0.0), axis=1).astype(jnp.int32)
    target = picked.T.reshape(-1) * CAP + slot
    slots = jnp.arange(SLOTS, dtype=jnp.int32)
    gather_q = (target[:, None] == slots[None, :]).astype(bf)
    spread_q = (slots[:, None] == target[None, :]).astype(bf)
    spread = spread_q[:, :NEW_DEV] + spread_q[:, NEW_DEV:]
    rows_send = jnp.dot(spread, normed, preferred_element_type=f32).astype(bf)
    both_gates = jnp.where(
        target[:NEW_DEV, None] == slots[None, :], gate_first[:, None], 0.0
    ) + jnp.where(target[NEW_DEV:, None] == slots[None, :], 1.0 - gate_first[:, None], 0.0)
    gates_high = both_gates.astype(bf)
    gates_low = (both_gates - gates_high.astype(f32)).astype(bf)
    gates = jnp.concatenate([gates_high, gates_low], axis=1)
    q_cos = jnp.concatenate([cosine[:NEW_DEV]] * 2, 0)
    q_sin = jnp.concatenate([sine[:NEW_DEV]] * 2, 0)
    mixed = layer(
        kv_own,
        bias_own,
        rows_send.reshape(EXPERTS, CAP, D),
        gather_q,
        spread_q,
        gates,
        q_cos,
        q_sin,
        tokens,
        w_query[0],
        w_out[0],
    )
    return mixed[None]


def solution(mesh):
    placed = (
        P("expert", "blk", None),
        P(),
        P(),
        P("expert", "blk", None),
        P("expert", None, None),
        P(),
        P(),
        P("expert", None, None),
        P("expert", "blk", None),
        P("expert", "blk", None),
        P("expert", "blk", None),
        P("expert", "blk"),
        P("expert", "blk"),
        P("expert"),
    )
    return jax.shard_map(
        shards, mesh=mesh, in_specs=placed, out_specs=P("expert", "blk", None), check_vma=False
    )
```

```python
import functools
import math

import jax
import jax.numpy as jnp
from jax import lax
from jax.experimental import pallas as pl
from jax.experimental.pallas import tpu as pltpu
from jax.sharding import PartitionSpec as P

HD = 128
KVH = 8
CB = 32
CAP = 64
D = 2048
KVW = KVH * HD
NEW_DEV = 128
CACHE_DEV = 320
KEYS = NEW_DEV + CACHE_DEV
HALF = KEYS // 2
EXPERTS = 8
SLOTS = EXPERTS * CAP
ROWS = 2 * NEW_DEV
KC = 4
KW = D // KC
NC = 4
NW = D // NC
NZ = 4

epsilon = 1e-06
theta_base = 10000.0
MASKED = -1e30
LOG2E = 1.4426950408889634
SCALE = LOG2E / math.sqrt(HD)


def normalize(hidden, norm_gain):
    widened = hidden.astype(jnp.float32)
    inverse = lax.rsqrt(jnp.mean(widened * widened, axis=-1, keepdims=True) + epsilon)
    return (widened * inverse * norm_gain).astype(jnp.bfloat16)


def rope_tables(positions):
    half_width = HD // 2
    frequency = jnp.exp(
        jnp.arange(half_width, dtype=jnp.float32) * (-math.log(theta_base) / half_width)
    )
    angles = positions.astype(jnp.float32)[:, None] * frequency[None, :]
    cosine = jnp.cos(angles)
    sine = jnp.sin(angles)
    return jnp.concatenate([cosine, cosine], 1), jnp.concatenate([-sine, sine], 1)


def rotate(projected, cosine, sine):
    row_count = projected.shape[0]
    half_width = HD // 2
    v = projected.reshape(row_count, KVH, HD)
    swapped = jnp.concatenate([v[..., half_width:], v[..., :half_width]], axis=-1)
    return v * cosine[:, None, :] + swapped * sine[:, None, :]


def product_nt(left, right):
    return lax.dot_general(
        left, right, (((1,), (1,)), ((), ())), preferred_element_type=jnp.float32
    )


def kernel(
    kv_own,
    bias_own,
    rows_send,
    gather_q,
    spread_q,
    gates,
    cosine,
    sine,
    tokens,
    w_query,
    w_out,
    out,
    kv,
    bias,
    rows,
    wq,
    wo,
    qacc,
    qsend,
    qret,
    queries,
    acc,
    own_part,
    num_send,
    num_recv,
    den_send,
    den_recv,
    att_send,
    att_recv,
    exp_send,
    exp_recv,
    local_sem,
    rows_s,
    rows_r,
    qs_s,
    qs_r,
    kv_s,
    kv_r,
    bias_s,
    bias_r,
    qx_s,
    qx_r,
    num_s,
    num_r,
    den_s,
    den_r,
    att_s,
    att_r,
    exp_s,
    exp_r,
):
    blk = lax.axis_index("blk")
    expert = lax.axis_index("expert")
    z = blk // 4
    xl = (blk // 2) % 2
    c = blk % 2
    xh = expert // 4
    y = expert % 4

    def at_blk(zz, xx, cc):
        return {"blk": zz * 4 + xx * 2 + cc, "expert": expert}

    def peer(off):
        return ((xh + off // 4) % 2) * 4 + (y + off % 4) % 4

    def at_expert(e):
        return {"blk": blk, "expert": e}

    zp = (z + 1) % NZ
    zm = (z + NZ - 1) % NZ
    zo = (z + 2) % NZ
    up = at_blk(zp, xl, c)
    down = at_blk(zm, xl, c)
    partner = at_blk(z, xl, 1 - c)
    across = at_blk(z, 1 - xl, c)
    mine = z * 2 + c

    def remote(src, dst, ssem, rsem, device):
        return pltpu.make_async_remote_copy(
            src_ref=src,
            dst_ref=dst,
            send_sem=ssem,
            recv_sem=rsem,
            device_id=device,
            device_id_type=pl.DeviceIdType.MESH,
        )

    barrier = pltpu.get_barrier_semaphore()
    for off in range(1, 8):
        pl.semaphore_signal(
            barrier, inc=1, device_id=at_expert(peer(off)), device_id_type=pl.DeviceIdType.MESH
        )
        pl.semaphore_signal(
            barrier,
            inc=1,
            device_id=at_blk((z + off // 2) % NZ, xl, (c + off % 2) % 2),
            device_id_type=pl.DeviceIdType.MESH,
        )
    pl.semaphore_signal(barrier, inc=1, device_id=across, device_id_type=pl.DeviceIdType.MESH)

    load_wq = pltpu.make_async_copy(w_query, wq, local_sem.at[0])
    load_wo = pltpu.make_async_copy(w_out, wo, local_sem.at[1])
    load_kv = pltpu.make_async_copy(kv_own, kv.at[:, mine], local_sem.at[2])
    load_wq.start()
    load_kv.start()
    load_wo.start()
    pl.semaphore_wait(barrier, 15)

    def rows_copy(k, off):
        e = peer(off)
        return remote(
            rows_send.at[e, :, pl.ds(pl.multiple_of(k * KW, KW), KW)],
            rows.at[k, expert],
            rows_s.at[k, off],
            rows_r.at[k, off],
            at_expert(e),
        )

    def rows_local(k):
        return pltpu.make_async_copy(
            rows_send.at[expert, :, pl.ds(pl.multiple_of(k * KW, KW), KW)],
            rows.at[k, expert],
            local_sem.at[3 + k],
        )

    def kv_own_copy(h, way):
        return remote(
            kv_own.at[h],
            kv.at[h, mine],
            kv_s.at[h, way],
            kv_r.at[h, way],
            (up, down, partner)[way],
        )

    def kv_forward(h, way):
        source = (zm, zp)[way] * 2 + c
        part = pl.ds(way * HALF, HALF)
        return remote(
            kv.at[h, source, part],
            kv.at[h, source, part],
            kv_s.at[h, 3 + way],
            kv_r.at[h, 3 + way],
            (up, down)[way],
        )

    def kv_share(h, which):
        if which < 2:
            ref = kv.at[h, (zm, zp)[which] * 2 + c]
        else:
            ref = kv.at[h, zo * 2 + c, pl.ds((which - 2) * HALF, HALF)]
        return remote(ref, ref, kv_s.at[h, 5 + which], kv_r.at[h, 5 + which], partner)

    def bias_copy(off):
        return remote(
            bias_own,
            bias.at[mine],
            bias_s.at[off],
            bias_r.at[off],
            at_blk((z + off // 2) % NZ, xl, (c + off % 2) % 2),
        )

    def send_rows(k, _):
        for off in range(1, 8):
            rows_copy(k, off).start()
        rows_local(k).start()
        return 0

    lax.fori_loop(0, KC, send_rows, 0)

    def send_kv(h, _):
        for way in range(3):
            kv_own_copy(h, way).start()
        return 0

    lax.fori_loop(0, KVH, send_kv, 0)
    for off in range(1, 8):
        bias_copy(off).start()
    bias[mine] = bias_own[...]

    load_wq.wait()

    def project(k, _):
        for off in range(1, 8):
            rows_copy(k, off).wait_recv()
        rows_local(k).wait()
        part = jnp.dot(
            rows[k].reshape(SLOTS, KW),
            wq[pl.ds(pl.multiple_of(k * KW, KW), KW), :],
            preferred_element_type=jnp.float32,
        )

        @pl.when(k == 0)
        def _():
            qacc[...] = part

        @pl.when(k > 0)
        def _():
            qacc[...] += part

        return 0

    lax.fori_loop(0, KC, project, 0)
    qsend[...] = qacc[...].astype(jnp.bfloat16).reshape(EXPERTS, CAP, KVW)

    def q_copy(off):
        r = peer(off)
        return remote(
            qsend.at[r], qret.at[expert], qs_s.at[off], qs_r.at[off], at_expert(r)
        )

    for off in range(1, 8):
        q_copy(off).start()
    q_local = pltpu.make_async_copy(qsend.at[expert], qret.at[expert], local_sem.at[7])
    q_local.start()

    def pass_on(h, _):
        for way in range(2):
            kv_own_copy(h, way).wait_recv()
            kv_forward(h, way).start()
        for way in range(2):
            kv_share(h, way).start()
        return 0

    lax.fori_loop(0, KVH, pass_on, 0)

    for off in range(1, 8):
        q_copy(off).wait_recv()
    q_local.wait()
    gathered = jnp.dot(
        gather_q[...], qret[...].reshape(SLOTS, KVW), preferred_element_type=jnp.float32
    )
    for h in range(KVH):
        v = gathered[:, h * HD : (h + 1) * HD]
        turned = v * cosine[...] + pltpu.roll(v, HD // 2, 1) * sine[...]
        queries[h, 0:ROWS] = turned.astype(jnp.bfloat16)

    def qx_copy(h):
        return remote(
            queries.at[h, pl.ds(0, ROWS)],
            queries.at[h, pl.ds(ROWS, ROWS)],
            qx_s.at[h],
            qx_r.at[h],
            across,
        )

    for h in range(KVH):
        qx_copy(h).start()
    for off in range(1, 8):
        bias_copy(off).wait_recv()
    load_kv.wait()

    lead = (
        lax.broadcasted_iota(jnp.int32, (ROWS, NEW_DEV), 0) % NEW_DEV
        - lax.broadcasted_iota(jnp.int32, (ROWS, NEW_DEV), 1)
    )

    def half(h, cc):
        old_part = slice(NEW_DEV, KEYS)
        blocks = [zz * 2 + cc for zz in range(NZ)]
        new_keys = jnp.concatenate([kv[h, j, 0:NEW_DEV, 0:HD] for j in blocks], axis=0)
        old_keys = jnp.concatenate([kv[h, j, old_part, 0:HD] for j in blocks], axis=0)
        new_scores = product_nt(queries[h], new_keys)
        old_scores = product_nt(queries[h], old_keys)
        shut = jnp.concatenate([bias[j, 0:1, 0:CACHE_DEV] for j in blocks], axis=1)
        pieces = []
        for zz, j in enumerate(blocks):
            offset_own = jnp.clip((j - mine) * NEW_DEV, -NEW_DEV, NEW_DEV)
            offset_across = jnp.clip(2 * (zz - z) + 2 * xl - 1, -1, 1) * NEW_DEV
            fresh = jnp.exp2(new_scores[:, zz * NEW_DEV : (zz + 1) * NEW_DEV] * SCALE)
            pieces.append(
                jnp.concatenate(
                    [
                        jnp.where(lead >= offset_own, fresh[0:ROWS], 0.0),
                        jnp.where(lead >= offset_across, fresh[ROWS:], 0.0),
                    ],
                    axis=0,
                ).astype(jnp.bfloat16)
            )
        pieces.append(jnp.exp2(old_scores * SCALE + shut).astype(jnp.bfloat16))
        values = jnp.concatenate(
            [kv[h, j, 0:NEW_DEV, HD : 2 * HD] for j in blocks]
            + [kv[h, j, old_part, HD : 2 * HD] for j in blocks],
            axis=0,
        )
        extended = jnp.concatenate([values, jnp.ones((NZ * KEYS, HD), jnp.bfloat16)], axis=1)
        return jnp.dot(
            jnp.concatenate(pieces, axis=1), extended, preferred_element_type=jnp.float32
        )

    def num_copy(h):
        return remote(num_send.at[h], num_recv.at[h], num_s.at[h], num_r.at[h], across)

    def den_copy(h):
        return remote(den_send.at[h], den_recv.at[h], den_s.at[h], den_r.at[h], across)

    def att_copy(h, off):
        e = peer(off)
        return remote(
            att_send.at[h, e],
            att_recv.at[h, expert],
            att_s.at[h, off],
            att_r.at[h, off],
            at_expert(e),
        )

    def att_local(h):
        return pltpu.make_async_copy(
            att_send.at[h, expert], att_recv.at[h, expert], local_sem.at[8 + h]
        )

    def finish(h):
        num_copy(h).wait_recv()
        den_copy(h).wait_recv()
        den_there = jnp.broadcast_to(den_recv[h][0:1, :], (HD, ROWS)).T
        numerator = own_part[h, :, 0:HD] + num_recv[h].astype(jnp.float32)
        denominator = own_part[h, :, HD:] + den_there
        attended = (numerator / denominator).astype(jnp.bfloat16)
        spread = jnp.dot(spread_q[...], attended, preferred_element_type=jnp.float32)
        att_send[h] = spread.astype(jnp.bfloat16).reshape(EXPERTS, CAP, HD)
        for off in range(1, 8):
            att_copy(h, off).start()
        att_local(h).start()

    def one_head(h, _):
        for way in range(2):
            kv_forward(h, way).wait_recv()
            kv_share(h, 2 + way).start()
        qx_copy(h).wait_recv()

        def side(i, _):
            @pl.when(i == 1)
            def _():
                kv_own_copy(h, 2).wait_recv()
                for which in range(4):
                    kv_share(h, which).wait_recv()

            part = half(h, (c + i) % 2)

            @pl.when(i == 0)
            def _():
                acc[...] = part

            @pl.when(i == 1)
            def _():
                acc[...] += part

            return 0

        lax.fori_loop(0, 2, side, 0)
        own_part[h] = acc[0:ROWS]
        num_send[h] = acc[ROWS:, 0:HD].astype(jnp.bfloat16)
        den_send[h] = acc[ROWS:, HD:].T[0:8, :]
        num_copy(h).start()
        den_copy(h).start()

        @pl.when(h >= 2)
        def _():
            finish(h - 2)

        return 0

    lax.fori_loop(0, KVH, one_head, 0)
    finish(KVH - 2)
    finish(KVH - 1)

    load_wo.wait()

    def wait_att(h, _):
        for off in range(1, 8):
            att_copy(h, off).wait_recv()
        att_local(h).wait()
        return 0

    lax.fori_loop(0, KVH, wait_att, 0)

    def exp_copy(n, off):
        r = peer(off)
        return remote(
            exp_send.at[n, r],
            exp_recv.at[n, expert],
            exp_s.at[n, off],
            exp_r.at[n, off],
            at_expert(r),
        )

    def exp_local(n):
        return pltpu.make_async_copy(
            exp_send.at[n, expert], exp_recv.at[n, expert], local_sem.at[16 + n]
        )

    arrived = jnp.concatenate([att_recv[h].reshape(SLOTS, HD) for h in range(KVH)], axis=1)

    def project_out(n, _):
        part = jnp.dot(
            arrived,
            wo[:, pl.ds(pl.multiple_of(n * NW, NW), NW)],
            preferred_element_type=jnp.float32,
        )
        exp_send[n] = part.astype(jnp.bfloat16).reshape(EXPERTS, CAP, NW)
        for off in range(1, 8):
            exp_copy(n, off).start()
        exp_local(n).start()
        return 0

    lax.fori_loop(0, NC, project_out, 0)

    def combine(n, _):
        for off in range(1, 8):
            exp_copy(n, off).wait_recv()
        exp_local(n).wait()
        back = exp_recv[n].reshape(SLOTS, NW)
        columns = pl.ds(pl.multiple_of(n * NW, NW), NW)
        mixed = jnp.dot(gates[:, 0:SLOTS], back, preferred_element_type=jnp.float32)
        mixed += jnp.dot(gates[:, SLOTS:], back, preferred_element_type=jnp.float32)
        out[:, columns] = (tokens[:, columns].astype(jnp.float32) + mixed).astype(jnp.bfloat16)
        return 0

    lax.fori_loop(0, NC, combine, 0)

    def drain_rows(k, _):
        for off in range(1, 8):
            rows_copy(k, off).wait_send()
            exp_copy(k, off).wait_send()
        return 0

    lax.fori_loop(0, KC, drain_rows, 0)

    def drain_heads(h, _):
        for way in range(3):
            kv_own_copy(h, way).wait_send()
        for way in range(2):
            kv_forward(h, way).wait_send()
        for which in range(4):
            kv_share(h, which).wait_send()
        qx_copy(h).wait_send()
        num_copy(h).wait_send()
        den_copy(h).wait_send()
        for off in range(1, 8):
            att_copy(h, off).wait_send()
        return 0

    lax.fori_loop(0, KVH, drain_heads, 0)
    for off in range(1, 8):
        bias_copy(off).wait_send()
        q_copy(off).wait_send()


def layer(kv_own, bias_own, rows_send, gather_q, spread_q, gates, cosine, sine, tokens, wq, wo):
    bf = jnp.bfloat16
    f32 = jnp.float32
    anywhere = pl.BlockSpec(memory_space=pl.ANY)
    inside = pl.BlockSpec(memory_space=pltpu.VMEM)
    dma = pltpu.SemaphoreType.DMA
    return pl.pallas_call(
        kernel,
        out_shape=jax.ShapeDtypeStruct((NEW_DEV, D), bf),
        in_specs=[anywhere, inside, anywhere] + [inside] * 6 + [anywhere] * 2,
        out_specs=inside,
        scratch_shapes=[
            pltpu.VMEM((KVH, 2 * NZ, KEYS, 2 * HD), bf),
            pltpu.VMEM((2 * NZ, 8, 384), f32),
            pltpu.VMEM((KC, EXPERTS, CAP, KW), bf),
            pltpu.VMEM((D, KVW), bf),
            pltpu.VMEM((KVW, D), bf),
            pltpu.VMEM((SLOTS, KVW), f32),
            pltpu.VMEM((EXPERTS, CAP, KVW), bf),
            pltpu.VMEM((EXPERTS, CAP, KVW), bf),
            pltpu.VMEM((KVH, 2 * ROWS, HD), bf),
            pltpu.VMEM((2 * ROWS, 2 * HD), f32),
            pltpu.VMEM((KVH, ROWS, 2 * HD), f32),
            pltpu.VMEM((KVH, ROWS, HD), bf),
            pltpu.VMEM((KVH, ROWS, HD), bf),
            pltpu.VMEM((KVH, 8, ROWS), f32),
            pltpu.VMEM((KVH, 8, ROWS), f32),
            pltpu.VMEM((KVH, EXPERTS, CAP, HD), bf),
            pltpu.VMEM((KVH, EXPERTS, CAP, HD), bf),
            pltpu.VMEM((NC, EXPERTS, CAP, NW), bf),
            pltpu.VMEM((NC, EXPERTS, CAP, NW), bf),
            dma((20,)),
            dma((KC, 8)),
            dma((KC, 8)),
            dma((8,)),
            dma((8,)),
            dma((KVH, 9)),
            dma((KVH, 9)),
            dma((8,)),
            dma((8,)),
            dma((KVH,)),
            dma((KVH,)),
            dma((KVH,)),
            dma((KVH,)),
            dma((KVH,)),
            dma((KVH,)),
            dma((KVH, 8)),
            dma((KVH, 8)),
            dma((NC, 8)),
            dma((NC, 8)),
        ],
        compiler_params=pltpu.CompilerParams(
            collective_id=0, has_side_effects=True, vmem_limit_bytes=60 * 1024 * 1024
        ),
        name="layer",
    )(kv_own, bias_own, rows_send, gather_q, spread_q, gates, cosine, sine, tokens, wq, wo)


def shards(
    new_tokens,
    norm_gain,
    router_weight,
    att_choice,
    w_query,
    w_key,
    w_value,
    w_out,
    cache_keys,
    cache_values,
    hidden_held,
    recompute_ids,
    block_live,
    cached_len,
):
    bf = jnp.bfloat16
    f32 = jnp.float32
    blk_index = lax.axis_index("blk")
    length = cached_len[0]
    tokens = new_tokens[0]
    normed = normalize(tokens, norm_gain)
    held_norm = normalize(hidden_held[0], norm_gain)
    new_pos = length + blk_index * NEW_DEV + jnp.arange(NEW_DEV, dtype=jnp.int32)
    held_start = recompute_ids[0, 0] * CB
    held_pos = blk_index * CACHE_DEV + held_start + jnp.arange(CB, dtype=jnp.int32)
    both_rows = jnp.concatenate([normed, held_norm], axis=0)
    cosine, sine = rope_tables(jnp.concatenate([new_pos, held_pos]))
    key_proj = rotate(
        jnp.dot(both_rows, w_key, preferred_element_type=f32), cosine, sine
    ).astype(bf)
    value_proj = (
        jnp.dot(both_rows, w_value, preferred_element_type=f32).astype(bf).reshape(-1, KVH, HD)
    )
    fresh = jnp.concatenate([key_proj, value_proj], axis=-1).transpose(1, 0, 2)
    cached = jnp.concatenate(
        [cache_keys[0].reshape(-1, KVH, HD), cache_values[0].reshape(-1, KVH, HD)], axis=-1
    ).transpose(1, 0, 2)
    kv_own = jnp.concatenate([fresh[:, :NEW_DEV], cached], axis=1)
    kv_own = lax.dynamic_update_slice(
        kv_own, fresh[:, NEW_DEV:], (0, NEW_DEV + held_start, 0)
    )
    slot_pos = blk_index * CACHE_DEV + jnp.arange(CACHE_DEV, dtype=jnp.int32)
    usable = (slot_pos < length) & (jnp.repeat(block_live[0], CB) == 1)
    bias_own = jnp.where(usable, 0.0, MASKED).astype(f32)
    bias_own = jnp.broadcast_to(jnp.pad(bias_own, (0, 384 - CACHE_DEV))[None], (8, 384))

    logits = jnp.dot(normed, router_weight, preferred_element_type=f32)
    picked = att_choice[0]
    ids = jnp.arange(EXPERTS, dtype=jnp.int32)
    one_hot = picked.T.reshape(-1)[:, None] == ids[None, :]
    chosen = jnp.sum(jnp.where(one_hot, jnp.concatenate([logits, logits], 0), 0.0), axis=1)
    gate_first = jax.nn.sigmoid(chosen[:NEW_DEV] - chosen[NEW_DEV:])
    order = jnp.arange(ROWS, dtype=jnp.int32)
    earlier = (order[:, None] > order[None, :]).astype(bf)
    before = jnp.dot(earlier, one_hot.astype(bf), preferred_element_type=f32)
    slot = jnp.sum(jnp.where(one_hot, before, 0.0), axis=1).astype(jnp.int32)
    target = picked.T.reshape(-1) * CAP + slot
    slots = jnp.arange(SLOTS, dtype=jnp.int32)
    gather_q = (target[:, None] == slots[None, :]).astype(bf)
    spread_q = (slots[:, None] == target[None, :]).astype(bf)
    spread = spread_q[:, :NEW_DEV] + spread_q[:, NEW_DEV:]
    rows_send = jnp.dot(spread, normed, preferred_element_type=f32).astype(bf)
    both_gates = jnp.where(
        target[:NEW_DEV, None] == slots[None, :], gate_first[:, None], 0.0
    ) + jnp.where(target[NEW_DEV:, None] == slots[None, :], 1.0 - gate_first[:, None], 0.0)
    gates_high = both_gates.astype(bf)
    gates_low = (both_gates - gates_high.astype(f32)).astype(bf)
    gates = jnp.concatenate([gates_high, gates_low], axis=1)
    q_cos = jnp.concatenate([cosine[:NEW_DEV]] * 2, 0)
    q_sin = jnp.concatenate([sine[:NEW_DEV]] * 2, 0)
    mixed = layer(
        kv_own,
        bias_own,
        rows_send.reshape(EXPERTS, CAP, D),
        gather_q,
        spread_q,
        gates,
        q_cos,
        q_sin,
        tokens,
        w_query[0],
        w_out[0],
    )
    return mixed[None]


def solution(mesh):
    placed = (
        P("expert", "blk", None),
        P(),
        P(),
        P("expert", "blk", None),
        P("expert", None, None),
        P(),
        P(),
        P("expert", None, None),
        P("expert", "blk", None),
        P("expert", "blk", None),
        P("expert", "blk", None),
        P("expert", "blk"),
        P("expert", "blk"),
        P("expert"),
    )
    return jax.shard_map(
        shards, mesh=mesh, in_specs=placed, out_specs=P("expert", "blk", None), check_vma=False
    )
```

```python
import math

import jax
import jax.numpy as jnp
import numpy as np
from jax import lax
from jax.experimental import pallas as pl
from jax.experimental.pallas import tpu as pltpu
from jax.sharding import PartitionSpec as P

HD = 128
KVH = 8
CB = 32
CAP = 64
D = 2048
KVW = KVH * HD
NEW_DEV = 128
CACHE_DEV = 320
KEYS = NEW_DEV + CACHE_DEV
HALF = KEYS // 2
EXPERTS = 8
SLOTS = EXPERTS * CAP
ROWS = 2 * NEW_DEV
KC = 4
KW = D // KC
NC = 4
NW = D // NC
NZ = 4
PAIRS = 4
PAIR = 2 * HD
BLK_DEV = 10
BIAS_WIDTH = 384

epsilon = 1e-06
theta_base = 10000.0
MASKED = -1e30
LOG2E = 1.4426950408889634
SCALE = LOG2E / math.sqrt(HD)


def product_nt(left, right):
    return lax.dot_general(
        left, right, (((1,), (1,)), ((), ())), preferred_element_type=jnp.float32
    )


def kernel(
    length_ref,
    held_ref,
    live_ref,
    tokens,
    hidden,
    gain,
    choice,
    router,
    base,
    step,
    w_key,
    w_value,
    cache_keys,
    cache_values,
    w_query,
    w_out,
    out,
    kv,
    bias,
    rows,
    wq,
    wo,
    qacc,
    qsend,
    qret,
    queries,
    acc,
    own_part,
    num_send,
    num_recv,
    den_send,
    den_recv,
    att_send,
    att_recv,
    exp_send,
    exp_recv,
    wk,
    wv,
    old_k,
    old_v,
    both,
    rows_send,
    bias_own,
    gather_q,
    spread_q,
    gates,
    cosine,
    sine,
    local_sem,
    rows_s,
    rows_r,
    qs_s,
    qs_r,
    kv_s,
    kv_r,
    bias_s,
    bias_r,
    qx_s,
    qx_r,
    num_s,
    num_r,
    den_s,
    den_r,
    att_s,
    att_r,
    exp_s,
    exp_r,
):
    blk = lax.axis_index("blk")
    expert = lax.axis_index("expert")
    z = blk // 4
    xl = (blk // 2) % 2
    c = blk % 2
    xh = expert // 4
    y = expert % 4

    def at_blk(zz, xx, cc):
        return {"blk": zz * 4 + xx * 2 + cc, "expert": expert}

    def peer(off):
        return ((xh + off // 4) % 2) * 4 + (y + off % 4) % 4

    def at_expert(e):
        return {"blk": blk, "expert": e}

    zp = (z + 1) % NZ
    zm = (z + NZ - 1) % NZ
    zo = (z + 2) % NZ
    up = at_blk(zp, xl, c)
    down = at_blk(zm, xl, c)
    partner = at_blk(z, xl, 1 - c)
    across = at_blk(z, 1 - xl, c)
    mine = z * 2 + c

    def remote(src, dst, ssem, rsem, device):
        return pltpu.make_async_remote_copy(
            src_ref=src,
            dst_ref=dst,
            send_sem=ssem,
            recv_sem=rsem,
            device_id=device,
            device_id_type=pl.DeviceIdType.MESH,
        )

    barrier = pltpu.get_barrier_semaphore()
    for off in range(1, 8):
        pl.semaphore_signal(
            barrier, inc=1, device_id=at_expert(peer(off)), device_id_type=pl.DeviceIdType.MESH
        )
        pl.semaphore_signal(
            barrier,
            inc=1,
            device_id=at_blk((z + off // 2) % NZ, xl, (c + off % 2) % 2),
            device_id_type=pl.DeviceIdType.MESH,
        )
    pl.semaphore_signal(barrier, inc=1, device_id=across, device_id_type=pl.DeviceIdType.MESH)

    load_wq = pltpu.make_async_copy(w_query, wq, local_sem.at[0])
    load_wo = pltpu.make_async_copy(w_out, wo, local_sem.at[1])

    def load_wk(p):
        columns = pl.ds(p * PAIR, PAIR)
        return pltpu.make_async_copy(w_key.at[:, columns], wk.at[p], local_sem.at[20 + p])

    def load_wv(p):
        columns = pl.ds(p * PAIR, PAIR)
        return pltpu.make_async_copy(w_value.at[:, columns], wv.at[p], local_sem.at[24 + p])

    load_old_k = pltpu.make_async_copy(cache_keys, old_k, local_sem.at[28])
    load_old_v = pltpu.make_async_copy(cache_values, old_v, local_sem.at[29])
    load_old_k.start()
    load_old_v.start()
    for p in range(PAIRS):
        load_wk(p).start()
        load_wv(p).start()
    load_wq.start()
    load_wo.start()

    def norm(hidden_rows):
        widened = hidden_rows.astype(jnp.float32)
        inverse = lax.rsqrt(jnp.mean(widened * widened, axis=-1, keepdims=True) + epsilon)
        return (widened * inverse * gain[...]).astype(jnp.bfloat16)

    both[0:NEW_DEV] = norm(tokens[...])
    both[NEW_DEV:] = norm(hidden[...])

    lane = lax.broadcasted_iota(jnp.int32, (NEW_DEV, HD), 1)
    row = lax.broadcasted_iota(jnp.int32, (NEW_DEV, HD), 0)
    earlier = (row > lane).astype(jnp.bfloat16)
    hot = [choice[:, k : k + 1] == lane for k in range(2)]
    count = [
        jnp.dot(earlier, jnp.where(m, 1.0, 0.0).astype(jnp.bfloat16), preferred_element_type=jnp.float32)
        for m in hot
    ]
    total = jnp.sum(jnp.where(hot[0], 1.0, 0.0), axis=0, keepdims=True)
    count[1] = count[1] + total
    slot_lane = lax.broadcasted_iota(jnp.int32, (NEW_DEV, SLOTS), 1)
    at_slot = []
    for k in range(2):
        slot = jnp.sum(jnp.where(hot[k], count[k], 0.0), axis=1, keepdims=True)
        target = choice[:, k : k + 1] * CAP + slot.astype(jnp.int32)
        at_slot.append(slot_lane == target)
    placed = [jnp.where(m, 1.0, 0.0) for m in at_slot]
    gather_q[0:NEW_DEV] = placed[0].astype(jnp.bfloat16)
    gather_q[NEW_DEV:] = placed[1].astype(jnp.bfloat16)
    spread = [m.T for m in placed]
    spread_q[:, 0:NEW_DEV] = spread[0].astype(jnp.bfloat16)
    spread_q[:, NEW_DEV:] = spread[1].astype(jnp.bfloat16)
    dispatch = (spread[0] + spread[1]).astype(jnp.bfloat16)
    for k in range(KC):
        rows_send[k] = (
            jnp.dot(
                dispatch,
                both[0:NEW_DEV, k * KW : (k + 1) * KW],
                preferred_element_type=jnp.float32,
            )
            .astype(jnp.bfloat16)
            .reshape(EXPERTS, CAP, KW)
        )

    def rows_copy(k, off):
        e = peer(off)
        return remote(
            rows_send.at[k, e],
            rows.at[k, expert],
            rows_s.at[k, off],
            rows_r.at[k, off],
            at_expert(e),
        )

    def rows_local(k):
        return pltpu.make_async_copy(
            rows_send.at[k, expert],
            rows.at[k, expert],
            local_sem.at[3 + k],
        )

    def kv_own_copy(h, way):
        return remote(
            kv.at[h, mine],
            kv.at[h, mine],
            kv_s.at[h, way],
            kv_r.at[h, way],
            (up, down, partner)[way],
        )

    def kv_forward(h, way):
        source = (zm, zp)[way] * 2 + c
        part = pl.ds(way * HALF, HALF)
        return remote(
            kv.at[h, source, part],
            kv.at[h, source, part],
            kv_s.at[h, 3 + way],
            kv_r.at[h, 3 + way],
            (up, down)[way],
        )

    def kv_share(h, which):
        if which < 2:
            ref = kv.at[h, (zm, zp)[which] * 2 + c]
        else:
            ref = kv.at[h, zo * 2 + c, pl.ds((which - 2) * HALF, HALF)]
        return remote(ref, ref, kv_s.at[h, 5 + which], kv_r.at[h, 5 + which], partner)

    def bias_copy(off):
        return remote(
            bias_own,
            bias.at[mine],
            bias_s.at[off],
            bias_r.at[off],
            at_blk((z + off // 2) % NZ, xl, (c + off % 2) % 2),
        )

    def send_rows(k, _):
        for off in range(1, 8):
            rows_copy(k, off).start()
        rows_local(k).start()
        return 0

    pl.semaphore_wait(barrier, 15)
    lax.fori_loop(0, KC, send_rows, 0)

    cb = base[0:1, :]
    sb = base[1:2, :]
    ch = base[2:3, :]
    sh = base[3:4, :]
    ct = step[0]
    st = step[1]
    sign = jnp.where(lax.broadcasted_iota(jnp.int32, (1, HD), 1) < HD // 2, -1.0, 1.0)
    cosine[0:NEW_DEV] = cb * ct - sb * st
    sine[0:NEW_DEV] = (sb * ct + cb * st) * sign
    cosine[NEW_DEV:] = ch * ct[0:CB] - sh * st[0:CB]
    sine[NEW_DEV:] = (sh * ct[0:CB] + ch * st[0:CB]) * sign
    place = lax.broadcasted_iota(jnp.int32, (8, BIAS_WIDTH), 1)
    live = jnp.zeros((8, BIAS_WIDTH), jnp.int32)
    for j in range(BLK_DEV):
        live = jnp.where(place // CB == j, live_ref[0, j], live)
    usable = (live == 1) & (blk * CACHE_DEV + place < length_ref[0])
    bias_own[...] = jnp.where(usable, 0.0, MASKED)
    bias[mine] = bias_own[...]

    load_old_k.wait()
    load_old_v.wait()
    held = lax.broadcasted_iota(jnp.int32, (CACHE_DEV, HD), 0) // CB == held_ref[0, 0]

    for p in range(PAIRS):
        load_wk(p).wait()
        load_wv(p).wait()
        keys = jnp.dot(both[...], wk[p], preferred_element_type=jnp.float32)
        values = jnp.dot(both[...], wv[p], preferred_element_type=jnp.float32)
        for i in range(2):
            h = 2 * p + i
            k_head = keys[:, i * HD : (i + 1) * HD]
            k_head = k_head * cosine[...] + pltpu.roll(k_head, HD // 2, 1) * sine[...]
            v_head = values[:, i * HD : (i + 1) * HD]
            for new, old, at in ((k_head, old_k, 0), (v_head, old_v, HD)):
                new = new.astype(jnp.bfloat16)
                kv[h, mine, 0:NEW_DEV, at : at + HD] = new[0:NEW_DEV]
                kv[h, mine, NEW_DEV:, at : at + HD] = jnp.where(
                    held,
                    jnp.concatenate([new[NEW_DEV:]] * BLK_DEV, axis=0),
                    old[:, h * HD : (h + 1) * HD],
                )
        for i in range(2):
            for way in range(3):
                kv_own_copy(2 * p + i, way).start()
    for off in range(1, 8):
        bias_copy(off).start()

    logits = jnp.dot(both[0:NEW_DEV], router[...], preferred_element_type=jnp.float32)
    chosen = [
        jnp.sum(jnp.where(m[:, 0:EXPERTS], logits, 0.0), axis=1, keepdims=True) for m in hot
    ]
    gate_first = jax.nn.sigmoid(chosen[0] - chosen[1])
    both_gates = jnp.where(at_slot[0], gate_first, 0.0) + jnp.where(
        at_slot[1], 1.0 - gate_first, 0.0
    )
    gates_high = both_gates.astype(jnp.bfloat16)
    gates[:, 0:SLOTS] = gates_high
    gates[:, SLOTS:] = (both_gates - gates_high.astype(jnp.float32)).astype(jnp.bfloat16)

    load_wq.wait()

    def project(k, _):
        for off in range(1, 8):
            rows_copy(k, off).wait_recv()
        rows_local(k).wait()
        part = jnp.dot(
            rows[k].reshape(SLOTS, KW),
            wq[pl.ds(pl.multiple_of(k * KW, KW), KW), :],
            preferred_element_type=jnp.float32,
        )

        @pl.when(k == 0)
        def _():
            qacc[...] = part

        @pl.when(k > 0)
        def _():
            qacc[...] += part

        return 0

    lax.fori_loop(0, KC, project, 0)
    qsend[...] = qacc[...].astype(jnp.bfloat16).reshape(EXPERTS, CAP, KVW)

    def q_copy(off):
        r = peer(off)
        return remote(
            qsend.at[r], qret.at[expert], qs_s.at[off], qs_r.at[off], at_expert(r)
        )

    for off in range(1, 8):
        q_copy(off).start()
    q_local = pltpu.make_async_copy(qsend.at[expert], qret.at[expert], local_sem.at[7])
    q_local.start()

    def pass_on(h, _):
        for way in range(2):
            kv_own_copy(h, way).wait_recv()
            kv_forward(h, way).start()
        for way in range(2):
            kv_share(h, way).start()
        return 0

    lax.fori_loop(0, KVH, pass_on, 0)

    for off in range(1, 8):
        q_copy(off).wait_recv()
    q_local.wait()
    gathered = jnp.dot(
        gather_q[...], qret[...].reshape(SLOTS, KVW), preferred_element_type=jnp.float32
    )
    for h in range(KVH):
        v = gathered[:, h * HD : (h + 1) * HD]
        cos_q = jnp.concatenate([cosine[0:NEW_DEV]] * 2, axis=0)
        sin_q = jnp.concatenate([sine[0:NEW_DEV]] * 2, axis=0)
        turned = v * cos_q + pltpu.roll(v, HD // 2, 1) * sin_q
        queries[h, 0:ROWS] = turned.astype(jnp.bfloat16)

    def qx_copy(h):
        return remote(
            queries.at[h, pl.ds(0, ROWS)],
            queries.at[h, pl.ds(ROWS, ROWS)],
            qx_s.at[h],
            qx_r.at[h],
            across,
        )

    for h in range(KVH):
        qx_copy(h).start()
    for off in range(1, 8):
        bias_copy(off).wait_recv()

    lead = (
        lax.broadcasted_iota(jnp.int32, (ROWS, NEW_DEV), 0) % NEW_DEV
        - lax.broadcasted_iota(jnp.int32, (ROWS, NEW_DEV), 1)
    )

    def half(h, cc):
        old_part = slice(NEW_DEV, KEYS)
        blocks = [zz * 2 + cc for zz in range(NZ)]
        new_keys = jnp.concatenate([kv[h, j, 0:NEW_DEV, 0:HD] for j in blocks], axis=0)
        old_keys = jnp.concatenate([kv[h, j, old_part, 0:HD] for j in blocks], axis=0)
        new_scores = product_nt(queries[h], new_keys)
        old_scores = product_nt(queries[h], old_keys)
        shut = jnp.concatenate([bias[j, 0:1, 0:CACHE_DEV] for j in blocks], axis=1)
        pieces = []
        for zz, j in enumerate(blocks):
            offset_own = jnp.clip((j - mine) * NEW_DEV, -NEW_DEV, NEW_DEV)
            offset_across = jnp.clip(2 * (zz - z) + 2 * xl - 1, -1, 1) * NEW_DEV
            fresh = jnp.exp2(new_scores[:, zz * NEW_DEV : (zz + 1) * NEW_DEV] * SCALE)
            pieces.append(
                jnp.concatenate(
                    [
                        jnp.where(lead >= offset_own, fresh[0:ROWS], 0.0),
                        jnp.where(lead >= offset_across, fresh[ROWS:], 0.0),
                    ],
                    axis=0,
                ).astype(jnp.bfloat16)
            )
        pieces.append(jnp.exp2(old_scores * SCALE + shut).astype(jnp.bfloat16))
        values = jnp.concatenate(
            [kv[h, j, 0:NEW_DEV, HD : 2 * HD] for j in blocks]
            + [kv[h, j, old_part, HD : 2 * HD] for j in blocks],
            axis=0,
        )
        extended = jnp.concatenate([values, jnp.ones((NZ * KEYS, HD), jnp.bfloat16)], axis=1)
        return jnp.dot(
            jnp.concatenate(pieces, axis=1), extended, preferred_element_type=jnp.float32
        )

    def num_copy(h):
        return remote(num_send.at[h], num_recv.at[h], num_s.at[h], num_r.at[h], across)

    def den_copy(h):
        return remote(den_send.at[h], den_recv.at[h], den_s.at[h], den_r.at[h], across)

    def att_copy(h, off):
        e = peer(off)
        return remote(
            att_send.at[h, e],
            att_recv.at[h, expert],
            att_s.at[h, off],
            att_r.at[h, off],
            at_expert(e),
        )

    def att_local(h):
        return pltpu.make_async_copy(
            att_send.at[h, expert], att_recv.at[h, expert], local_sem.at[8 + h]
        )

    def finish(h):
        num_copy(h).wait_recv()
        den_copy(h).wait_recv()
        den_there = jnp.broadcast_to(den_recv[h][0:1, :], (HD, ROWS)).T
        numerator = own_part[h, :, 0:HD] + num_recv[h].astype(jnp.float32)
        denominator = own_part[h, :, HD:] + den_there
        attended = (numerator / denominator).astype(jnp.bfloat16)
        spread = jnp.dot(spread_q[...], attended, preferred_element_type=jnp.float32)
        att_send[h] = spread.astype(jnp.bfloat16).reshape(EXPERTS, CAP, HD)
        for off in range(1, 8):
            att_copy(h, off).start()
        att_local(h).start()

    def one_head(h, _):
        for way in range(2):
            kv_forward(h, way).wait_recv()
            kv_share(h, 2 + way).start()
        qx_copy(h).wait_recv()

        def side(i, _):
            @pl.when(i == 1)
            def _():
                kv_own_copy(h, 2).wait_recv()
                for which in range(4):
                    kv_share(h, which).wait_recv()

            part = half(h, (c + i) % 2)

            @pl.when(i == 0)
            def _():
                acc[...] = part

            @pl.when(i == 1)
            def _():
                acc[...] += part

            return 0

        lax.fori_loop(0, 2, side, 0)
        own_part[h] = acc[0:ROWS]
        num_send[h] = acc[ROWS:, 0:HD].astype(jnp.bfloat16)
        den_send[h] = acc[ROWS:, HD:].T[0:8, :]
        num_copy(h).start()
        den_copy(h).start()

        @pl.when(h >= 2)
        def _():
            finish(h - 2)

        return 0

    lax.fori_loop(0, KVH, one_head, 0)
    finish(KVH - 2)
    finish(KVH - 1)

    load_wo.wait()

    def wait_att(h, _):
        for off in range(1, 8):
            att_copy(h, off).wait_recv()
        att_local(h).wait()
        return 0

    lax.fori_loop(0, KVH, wait_att, 0)

    def exp_copy(n, off):
        r = peer(off)
        return remote(
            exp_send.at[n, r],
            exp_recv.at[n, expert],
            exp_s.at[n, off],
            exp_r.at[n, off],
            at_expert(r),
        )

    def exp_local(n):
        return pltpu.make_async_copy(
            exp_send.at[n, expert], exp_recv.at[n, expert], local_sem.at[16 + n]
        )

    arrived = jnp.concatenate([att_recv[h].reshape(SLOTS, HD) for h in range(KVH)], axis=1)

    def project_out(n, _):
        part = jnp.dot(
            arrived,
            wo[:, pl.ds(pl.multiple_of(n * NW, NW), NW)],
            preferred_element_type=jnp.float32,
        )
        exp_send[n] = part.astype(jnp.bfloat16).reshape(EXPERTS, CAP, NW)
        for off in range(1, 8):
            exp_copy(n, off).start()
        exp_local(n).start()
        return 0

    lax.fori_loop(0, NC, project_out, 0)

    def combine(n, _):
        for off in range(1, 8):
            exp_copy(n, off).wait_recv()
        exp_local(n).wait()
        back = exp_recv[n].reshape(SLOTS, NW)
        columns = pl.ds(pl.multiple_of(n * NW, NW), NW)
        mixed = jnp.dot(gates[:, 0:SLOTS], back, preferred_element_type=jnp.float32)
        mixed += jnp.dot(gates[:, SLOTS:], back, preferred_element_type=jnp.float32)
        out[:, columns] = (tokens[:, columns].astype(jnp.float32) + mixed).astype(jnp.bfloat16)
        return 0

    lax.fori_loop(0, NC, combine, 0)

    def drain_rows(k, _):
        for off in range(1, 8):
            rows_copy(k, off).wait_send()
            exp_copy(k, off).wait_send()
        return 0

    lax.fori_loop(0, KC, drain_rows, 0)

    def drain_heads(h, _):
        for way in range(3):
            kv_own_copy(h, way).wait_send()
        for way in range(2):
            kv_forward(h, way).wait_send()
        for which in range(4):
            kv_share(h, which).wait_send()
        qx_copy(h).wait_send()
        num_copy(h).wait_send()
        den_copy(h).wait_send()
        for off in range(1, 8):
            att_copy(h, off).wait_send()
        return 0

    lax.fori_loop(0, KVH, drain_heads, 0)
    for off in range(1, 8):
        bias_copy(off).wait_send()
        q_copy(off).wait_send()


def layer(*operands):
    bf = jnp.bfloat16
    f32 = jnp.float32
    anywhere = pl.BlockSpec(memory_space=pl.ANY)
    inside = pl.BlockSpec(memory_space=pltpu.VMEM)
    scalars = pl.BlockSpec(memory_space=pltpu.SMEM)
    dma = pltpu.SemaphoreType.DMA
    return pl.pallas_call(
        kernel,
        out_shape=jax.ShapeDtypeStruct((NEW_DEV, D), bf),
        in_specs=[scalars] * 3 + [inside] * 7 + [anywhere] * 6,
        out_specs=inside,
        scratch_shapes=[
            pltpu.VMEM((KVH, 2 * NZ, KEYS, 2 * HD), bf),
            pltpu.VMEM((2 * NZ, 8, BIAS_WIDTH), f32),
            pltpu.VMEM((KC, EXPERTS, CAP, KW), bf),
            pltpu.VMEM((D, KVW), bf),
            pltpu.VMEM((KVW, D), bf),
            pltpu.VMEM((SLOTS, KVW), f32),
            pltpu.VMEM((EXPERTS, CAP, KVW), bf),
            pltpu.VMEM((EXPERTS, CAP, KVW), bf),
            pltpu.VMEM((KVH, 2 * ROWS, HD), bf),
            pltpu.VMEM((2 * ROWS, 2 * HD), f32),
            pltpu.VMEM((KVH, ROWS, 2 * HD), f32),
            pltpu.VMEM((KVH, ROWS, HD), bf),
            pltpu.VMEM((KVH, ROWS, HD), bf),
            pltpu.VMEM((KVH, 8, ROWS), f32),
            pltpu.VMEM((KVH, 8, ROWS), f32),
            pltpu.VMEM((KVH, EXPERTS, CAP, HD), bf),
            pltpu.VMEM((KVH, EXPERTS, CAP, HD), bf),
            pltpu.VMEM((NC, EXPERTS, CAP, NW), bf),
            pltpu.VMEM((NC, EXPERTS, CAP, NW), bf),
            pltpu.VMEM((PAIRS, D, PAIR), bf),
            pltpu.VMEM((PAIRS, D, PAIR), bf),
            pltpu.VMEM((CACHE_DEV, KVW), bf),
            pltpu.VMEM((CACHE_DEV, KVW), bf),
            pltpu.VMEM((NEW_DEV + CB, D), bf),
            pltpu.VMEM((KC, EXPERTS, CAP, KW), bf),
            pltpu.VMEM((8, BIAS_WIDTH), f32),
            pltpu.VMEM((ROWS, SLOTS), bf),
            pltpu.VMEM((SLOTS, ROWS), bf),
            pltpu.VMEM((NEW_DEV, 2 * SLOTS), bf),
            pltpu.VMEM((NEW_DEV + CB, HD), f32),
            pltpu.VMEM((NEW_DEV + CB, HD), f32),
            dma((32,)),
            dma((KC, 8)),
            dma((KC, 8)),
            dma((8,)),
            dma((8,)),
            dma((KVH, 9)),
            dma((KVH, 9)),
            dma((8,)),
            dma((8,)),
            dma((KVH,)),
            dma((KVH,)),
            dma((KVH,)),
            dma((KVH,)),
            dma((KVH,)),
            dma((KVH,)),
            dma((KVH, 8)),
            dma((KVH, 8)),
            dma((NC, 8)),
            dma((NC, 8)),
        ],
        compiler_params=pltpu.CompilerParams(
            collective_id=0, has_side_effects=True, vmem_limit_bytes=63 * 1024 * 1024
        ),
        name="layer",
    )(*operands)


def shards(
    new_tokens,
    norm_gain,
    router_weight,
    att_choice,
    w_query,
    w_key,
    w_value,
    w_out,
    cache_keys,
    cache_values,
    hidden_held,
    recompute_ids,
    block_live,
    cached_len,
):
    blk_index = lax.axis_index("blk")
    frequency = jnp.exp(
        (jnp.arange(HD, dtype=jnp.int32) % (HD // 2)).astype(jnp.float32)
        * (-math.log(theta_base) / (HD // 2))
    )
    new_base = (cached_len[0] + blk_index * NEW_DEV).astype(jnp.float32) * frequency
    held_base = (blk_index * CACHE_DEV + recompute_ids[0, 0] * CB).astype(jnp.float32) * frequency
    angles = jnp.stack([new_base, new_base, held_base, held_base])
    odd = jnp.arange(4)[:, None] % 2 == 1
    base = jnp.where(odd, jnp.sin(angles), jnp.cos(angles))
    wave = np.exp((np.arange(HD) % (HD // 2)) * (-math.log(theta_base) / (HD // 2)))
    turns = np.arange(NEW_DEV)[:, None] * wave[None, :]
    step = jnp.asarray(np.stack([np.cos(turns), np.sin(turns)]), jnp.float32)
    mixed = layer(
        cached_len,
        recompute_ids,
        block_live,
        new_tokens[0],
        hidden_held[0],
        norm_gain[None, :],
        att_choice[0],
        router_weight,
        base,
        step,
        w_key,
        w_value,
        cache_keys[0],
        cache_values[0],
        w_query[0],
        w_out[0],
    )
    return mixed[None]


def solution(mesh):
    placed = (
        P("expert", "blk", None),
        P(),
        P(),
        P("expert", "blk", None),
        P("expert", None, None),
        P(),
        P(),
        P("expert", None, None),
        P("expert", "blk", None),
        P("expert", "blk", None),
        P("expert", "blk", None),
        P("expert", "blk"),
        P("expert", "blk"),
        P("expert"),
    )
    return jax.shard_map(
        shards, mesh=mesh, in_specs=placed, out_specs=P("expert", "blk", None), check_vma=False
    )
```

```python
import math

import jax
import jax.numpy as jnp
import numpy as np
from jax import lax
from jax.experimental import pallas as pl
from jax.experimental.pallas import tpu as pltpu
from jax.sharding import PartitionSpec as P

HD = 128
KVH = 8
CB = 32
CAP = 64
D = 2048
KVW = KVH * HD
NEW_DEV = 128
CACHE_DEV = 320
KEYS = NEW_DEV + CACHE_DEV
HALF = KEYS // 2
EXPERTS = 8
SLOTS = EXPERTS * CAP
ROWS = 2 * NEW_DEV
KC = 4
KW = D // KC
NC = 4
NW = D // NC
NZ = 4
PAIRS = 4
PAIR = 2 * HD
BLK_DEV = 10
BIAS_WIDTH = 384
EARLY = 6
PASS_AT = (3, 4, 5, 6, 7)

epsilon = 1e-06
theta_base = 10000.0
MASKED = -1e30
LOG2E = 1.4426950408889634
SCALE = LOG2E / math.sqrt(HD)


def product_nt(left, right):
    return lax.dot_general(
        left, right, (((1,), (1,)), ((), ())), preferred_element_type=jnp.float32
    )


def kernel(
    length_ref,
    held_ref,
    live_ref,
    tokens,
    hidden,
    gain,
    choice,
    router,
    base,
    step,
    w_key,
    w_value,
    cache_keys,
    cache_values,
    w_query,
    w_out,
    out,
    kv,
    bias,
    rows,
    wq,
    wo,
    qacc,
    qsend,
    qret,
    queries,
    acc,
    own_part,
    num_send,
    num_recv,
    den_send,
    den_recv,
    att_send,
    att_recv,
    exp_send,
    exp_recv,
    out_acc,
    wk,
    wv,
    old_k,
    old_v,
    both,
    rows_send,
    bias_own,
    gather_q,
    spread_q,
    gates,
    cosine,
    sine,
    local_sem,
    rows_s,
    rows_r,
    qs_s,
    qs_r,
    kv_s,
    kv_r,
    bias_s,
    bias_r,
    qx_s,
    qx_r,
    num_s,
    num_r,
    den_s,
    den_r,
    att_s,
    att_r,
    exp_s,
    exp_r,
):
    blk = lax.axis_index("blk")
    expert = lax.axis_index("expert")
    z = blk // 4
    xl = (blk // 2) % 2
    c = blk % 2
    xh = expert // 4
    y = expert % 4

    def at_blk(zz, xx, cc):
        return {"blk": zz * 4 + xx * 2 + cc, "expert": expert}

    def peer(off):
        return ((xh + off // 4) % 2) * 4 + (y + off % 4) % 4

    def at_expert(e):
        return {"blk": blk, "expert": e}

    zp = (z + 1) % NZ
    zm = (z + NZ - 1) % NZ
    zo = (z + 2) % NZ
    up = at_blk(zp, xl, c)
    down = at_blk(zm, xl, c)
    partner = at_blk(z, xl, 1 - c)
    across = at_blk(z, 1 - xl, c)
    mine = z * 2 + c

    def remote(src, dst, ssem, rsem, device):
        return pltpu.make_async_remote_copy(
            src_ref=src,
            dst_ref=dst,
            send_sem=ssem,
            recv_sem=rsem,
            device_id=device,
            device_id_type=pl.DeviceIdType.MESH,
        )

    barrier = pltpu.get_barrier_semaphore()
    for off in range(1, 8):
        pl.semaphore_signal(
            barrier, inc=1, device_id=at_expert(peer(off)), device_id_type=pl.DeviceIdType.MESH
        )
        pl.semaphore_signal(
            barrier,
            inc=1,
            device_id=at_blk((z + off // 2) % NZ, xl, (c + off % 2) % 2),
            device_id_type=pl.DeviceIdType.MESH,
        )
    pl.semaphore_signal(barrier, inc=1, device_id=across, device_id_type=pl.DeviceIdType.MESH)

    load_wq = pltpu.make_async_copy(w_query, wq, local_sem.at[0])
    load_wo = pltpu.make_async_copy(w_out, wo, local_sem.at[1])

    def load_wk(p):
        columns = pl.ds(p * PAIR, PAIR)
        return pltpu.make_async_copy(w_key.at[:, columns], wk.at[p], local_sem.at[20 + p])

    def load_wv(p):
        columns = pl.ds(p * PAIR, PAIR)
        return pltpu.make_async_copy(w_value.at[:, columns], wv.at[p], local_sem.at[24 + p])

    load_old_k = pltpu.make_async_copy(cache_keys, old_k, local_sem.at[28])
    load_old_v = pltpu.make_async_copy(cache_values, old_v, local_sem.at[29])
    load_old_k.start()
    load_old_v.start()
    for p in range(PAIRS):
        load_wk(p).start()
        load_wv(p).start()
    load_wq.start()
    load_wo.start()

    def norm(hidden_rows):
        widened = hidden_rows.astype(jnp.float32)
        inverse = lax.rsqrt(jnp.mean(widened * widened, axis=-1, keepdims=True) + epsilon)
        return (widened * inverse * gain[...]).astype(jnp.bfloat16)

    both[0:NEW_DEV] = norm(tokens[...])
    both[NEW_DEV:] = norm(hidden[...])

    def rows_copy(k, off):
        e = peer(off)
        return remote(
            rows_send.at[k, e],
            rows.at[k, expert],
            rows_s.at[k, off],
            rows_r.at[k, off],
            at_expert(e),
        )

    def rows_local(k):
        return pltpu.make_async_copy(
            rows_send.at[k, expert],
            rows.at[k, expert],
            local_sem.at[3 + k],
        )

    def kv_own_copy(h, way):
        return remote(
            kv.at[h, mine],
            kv.at[h, mine],
            kv_s.at[h, way],
            kv_r.at[h, way],
            (up, down, partner)[way],
        )

    def kv_forward(h, way):
        source = (zm, zp)[way] * 2 + c
        part = pl.ds(way * HALF, HALF)
        return remote(
            kv.at[h, source, part],
            kv.at[h, source, part],
            kv_s.at[h, 3 + way],
            kv_r.at[h, 3 + way],
            (up, down)[way],
        )

    def kv_share(h, which):
        if which < 2:
            ref = kv.at[h, (zm, zp)[which] * 2 + c]
        else:
            ref = kv.at[h, zo * 2 + c, pl.ds((which - 2) * HALF, HALF)]
        return remote(ref, ref, kv_s.at[h, 5 + which], kv_r.at[h, 5 + which], partner)

    def bias_copy(off):
        return remote(
            bias_own,
            bias.at[mine],
            bias_s.at[off],
            bias_r.at[off],
            at_blk((z + off // 2) % NZ, xl, (c + off % 2) % 2),
        )

    cb = base[0:1, :]
    sb = base[1:2, :]
    ch = base[2:3, :]
    sh = base[3:4, :]
    ct = step[0]
    st = step[1]
    sign = jnp.where(lax.broadcasted_iota(jnp.int32, (1, HD), 1) < HD // 2, -1.0, 1.0)
    cosine[0:NEW_DEV] = cb * ct - sb * st
    sine[0:NEW_DEV] = (sb * ct + cb * st) * sign
    cosine[NEW_DEV:] = ch * ct[0:CB] - sh * st[0:CB]
    sine[NEW_DEV:] = (sh * ct[0:CB] + ch * st[0:CB]) * sign
    place = lax.broadcasted_iota(jnp.int32, (8, BIAS_WIDTH), 1)
    live = jnp.zeros((8, BIAS_WIDTH), jnp.int32)
    for j in range(BLK_DEV):
        live = jnp.where(place // CB == j, live_ref[0, j], live)
    usable = (live == 1) & (blk * CACHE_DEV + place < length_ref[0])
    bias_own[...] = jnp.where(usable, 0.0, MASKED)
    bias[mine] = bias_own[...]

    load_old_k.wait()
    load_old_v.wait()
    held = lax.broadcasted_iota(jnp.int32, (CACHE_DEV, HD), 0) // CB == held_ref[0, 0]

    def own_pair(p):
        load_wk(p).wait()
        load_wv(p).wait()
        keys = jnp.dot(both[...], wk[p], preferred_element_type=jnp.float32)
        values = jnp.dot(both[...], wv[p], preferred_element_type=jnp.float32)
        for i in range(2):
            h = 2 * p + i
            k_head = keys[:, i * HD : (i + 1) * HD]
            k_head = k_head * cosine[...] + pltpu.roll(k_head, HD // 2, 1) * sine[...]
            v_head = values[:, i * HD : (i + 1) * HD]
            for new, old, at in ((k_head, old_k, 0), (v_head, old_v, HD)):
                new = new.astype(jnp.bfloat16)
                kv[h, mine, 0:NEW_DEV, at : at + HD] = new[0:NEW_DEV]
                kv[h, mine, NEW_DEV:, at : at + HD] = jnp.where(
                    held,
                    jnp.concatenate([new[NEW_DEV:]] * BLK_DEV, axis=0),
                    old[:, h * HD : (h + 1) * HD],
                )

    def send_pair(p):
        for i in range(2):
            for way in range(3):
                kv_own_copy(2 * p + i, way).start()

    own_pair(0)
    pl.semaphore_wait(barrier, 15)
    send_pair(0)

    lane = lax.broadcasted_iota(jnp.int32, (NEW_DEV, HD), 1)
    row = lax.broadcasted_iota(jnp.int32, (NEW_DEV, HD), 0)
    earlier = (row > lane).astype(jnp.bfloat16)
    named = [
        jnp.broadcast_to(choice[k : k + 1, :].astype(jnp.float32), (HD, NEW_DEV)).T.astype(jnp.int32)
        for k in range(2)
    ]
    hot = [named[k] == lane for k in range(2)]
    count = [
        jnp.dot(earlier, jnp.where(m, 1.0, 0.0).astype(jnp.bfloat16), preferred_element_type=jnp.float32)
        for m in hot
    ]
    total = jnp.sum(jnp.where(hot[0], 1.0, 0.0), axis=0, keepdims=True)
    count[1] = count[1] + total
    slot_lane = lax.broadcasted_iota(jnp.int32, (NEW_DEV, SLOTS), 1)
    at_slot = []
    for k in range(2):
        slot = jnp.sum(jnp.where(hot[k], count[k], 0.0), axis=1, keepdims=True)
        target = named[k][:, 0:1] * CAP + slot.astype(jnp.int32)
        at_slot.append(slot_lane == target)
    placed = [jnp.where(m, 1.0, 0.0) for m in at_slot]
    gather_q[0:NEW_DEV] = placed[0].astype(jnp.bfloat16)
    gather_q[NEW_DEV:] = placed[1].astype(jnp.bfloat16)
    spread = [m.T for m in placed]
    spread_q[:, 0:NEW_DEV] = spread[0].astype(jnp.bfloat16)
    spread_q[:, NEW_DEV:] = spread[1].astype(jnp.bfloat16)
    dispatch = (spread[0] + spread[1]).astype(jnp.bfloat16)
    for k in range(KC):
        rows_send[k] = (
            jnp.dot(
                dispatch,
                both[0:NEW_DEV, k * KW : (k + 1) * KW],
                preferred_element_type=jnp.float32,
            )
            .astype(jnp.bfloat16)
            .reshape(EXPERTS, CAP, KW)
        )

    def send_rows(k, _):
        for off in range(1, 8):
            rows_copy(k, off).start()
        rows_local(k).start()
        return 0

    lax.fori_loop(0, KC, send_rows, 0)

    for p in range(1, PAIRS):
        own_pair(p)
        send_pair(p)
    for off in range(1, 8):
        bias_copy(off).start()

    logits = product_nt(both[0:NEW_DEV], router[...])
    chosen = [
        jnp.sum(jnp.where(m[:, 0:EXPERTS], logits, 0.0), axis=1, keepdims=True) for m in hot
    ]
    gate_first = jax.nn.sigmoid(chosen[0] - chosen[1])
    both_gates = jnp.where(at_slot[0], gate_first, 0.0) + jnp.where(
        at_slot[1], 1.0 - gate_first, 0.0
    )
    gates_high = both_gates.astype(jnp.bfloat16)
    gates[:, 0:SLOTS] = gates_high
    gates[:, SLOTS:] = (both_gates - gates_high.astype(jnp.float32)).astype(jnp.bfloat16)

    def pass_on(h, _):
        for way in range(2):
            kv_own_copy(h, way).wait_recv()
            kv_forward(h, way).start()
        for way in range(2):
            kv_share(h, way).start()
        return 0

    load_wq.wait()

    def project(k, _):
        for off in range(1, 8):
            rows_copy(k, off).wait_recv()
        rows_local(k).wait()

        @pl.when(k > 0)
        def _():
            pass_on(k - 1, 0)

        part = jnp.dot(
            rows[k].reshape(SLOTS, KW),
            wq[pl.ds(pl.multiple_of(k * KW, KW), KW), :],
            preferred_element_type=jnp.float32,
        )

        @pl.when(k == 0)
        def _():
            qacc[...] = part

        @pl.when(k > 0)
        def _():
            qacc[...] += part

        return 0

    lax.fori_loop(0, KC, project, 0)

    def q_copy(p, off):
        r = peer(off)
        return remote(
            qsend.at[p, r], qret.at[p, expert], qs_s.at[p, off], qs_r.at[p, off], at_expert(r)
        )

    def q_local(p):
        return pltpu.make_async_copy(
            qsend.at[p, expert], qret.at[p, expert], local_sem.at[30 + p]
        )

    for p in range(PAIRS):
        qsend[p] = (
            qacc[:, p * PAIR : (p + 1) * PAIR].astype(jnp.bfloat16).reshape(EXPERTS, CAP, PAIR)
        )
        for off in range(1, 8):
            q_copy(p, off).start()
        q_local(p).start()

    def qx_copy(h):
        return remote(
            queries.at[h, pl.ds(0, ROWS)],
            queries.at[h, pl.ds(ROWS, ROWS)],
            qx_s.at[h],
            qx_r.at[h],
            across,
        )

    cos_q = jnp.concatenate([cosine[0:NEW_DEV]] * 2, axis=0)
    sin_q = jnp.concatenate([sine[0:NEW_DEV]] * 2, axis=0)
    for p in range(PAIRS):
        lax.fori_loop(PASS_AT[p], PASS_AT[p + 1], pass_on, 0)
        for off in range(1, 8):
            q_copy(p, off).wait_recv()
        q_local(p).wait()
        gathered = jnp.dot(
            gather_q[...], qret[p].reshape(SLOTS, PAIR), preferred_element_type=jnp.float32
        )
        for i in range(2):
            v = gathered[:, i * HD : (i + 1) * HD]
            turned = v * cos_q + pltpu.roll(v, HD // 2, 1) * sin_q
            queries[2 * p + i, 0:ROWS] = turned.astype(jnp.bfloat16)
        for i in range(2):
            qx_copy(2 * p + i).start()
    lax.fori_loop(PASS_AT[PAIRS], KVH, pass_on, 0)
    for off in range(1, 8):
        bias_copy(off).wait_recv()

    lead = (
        lax.broadcasted_iota(jnp.int32, (ROWS, NEW_DEV), 0) % NEW_DEV
        - lax.broadcasted_iota(jnp.int32, (ROWS, NEW_DEV), 1)
    )

    def half(h, cc):
        old_part = slice(NEW_DEV, KEYS)
        blocks = [zz * 2 + cc for zz in range(NZ)]
        new_keys = jnp.concatenate([kv[h, j, 0:NEW_DEV, 0:HD] for j in blocks], axis=0)
        old_keys = jnp.concatenate([kv[h, j, old_part, 0:HD] for j in blocks], axis=0)
        new_scores = product_nt(queries[h], new_keys)
        old_scores = product_nt(queries[h], old_keys)
        shut = jnp.concatenate([bias[j, 0:1, 0:CACHE_DEV] for j in blocks], axis=1)
        pieces = []
        for zz, j in enumerate(blocks):
            offset_own = jnp.clip((j - mine) * NEW_DEV, -NEW_DEV, NEW_DEV)
            offset_across = jnp.clip(2 * (zz - z) + 2 * xl - 1, -1, 1) * NEW_DEV
            fresh = jnp.exp2(new_scores[:, zz * NEW_DEV : (zz + 1) * NEW_DEV] * SCALE)
            pieces.append(
                jnp.concatenate(
                    [
                        jnp.where(lead >= offset_own, fresh[0:ROWS], 0.0),
                        jnp.where(lead >= offset_across, fresh[ROWS:], 0.0),
                    ],
                    axis=0,
                ).astype(jnp.bfloat16)
            )
        pieces.append(jnp.exp2(old_scores * SCALE + shut).astype(jnp.bfloat16))
        values = jnp.concatenate(
            [kv[h, j, 0:NEW_DEV, HD : 2 * HD] for j in blocks]
            + [kv[h, j, old_part, HD : 2 * HD] for j in blocks],
            axis=0,
        )
        extended = jnp.concatenate([values, jnp.ones((NZ * KEYS, HD), jnp.bfloat16)], axis=1)
        return jnp.dot(
            jnp.concatenate(pieces, axis=1), extended, preferred_element_type=jnp.float32
        )

    def num_copy(h):
        return remote(num_send.at[h], num_recv.at[h], num_s.at[h], num_r.at[h], across)

    def den_copy(h):
        return remote(den_send.at[h], den_recv.at[h], den_s.at[h], den_r.at[h], across)

    def att_copy(h, off):
        e = peer(off)
        return remote(
            att_send.at[h, e],
            att_recv.at[h, expert],
            att_s.at[h, off],
            att_r.at[h, off],
            at_expert(e),
        )

    def att_local(h):
        return pltpu.make_async_copy(
            att_send.at[h, expert], att_recv.at[h, expert], local_sem.at[8 + h]
        )

    def finish(h):
        num_copy(h).wait_recv()
        den_copy(h).wait_recv()
        den_there = jnp.broadcast_to(den_recv[h][0:1, :], (HD, ROWS)).T
        numerator = own_part[h, :, 0:HD] + num_recv[h].astype(jnp.float32)
        denominator = own_part[h, :, HD:] + den_there
        attended = (numerator / denominator).astype(jnp.bfloat16)
        spread = jnp.dot(spread_q[...], attended, preferred_element_type=jnp.float32)
        att_send[h] = spread.astype(jnp.bfloat16).reshape(EXPERTS, CAP, HD)
        for off in range(1, 8):
            att_copy(h, off).start()
        att_local(h).start()

    def one_head(h, _):
        for way in range(2):
            kv_forward(h, way).wait_recv()
            kv_share(h, 2 + way).start()
        qx_copy(h).wait_recv()

        def side(i, _):
            @pl.when(i == 1)
            def _():
                kv_own_copy(h, 2).wait_recv()
                for which in range(4):
                    kv_share(h, which).wait_recv()

            part = half(h, (c + i) % 2)

            @pl.when(i == 0)
            def _():
                acc[...] = part

            @pl.when(i == 1)
            def _():
                acc[...] += part

            return 0

        lax.fori_loop(0, 2, side, 0)
        own_part[h] = acc[0:ROWS]
        num_send[h] = acc[ROWS:, 0:HD].astype(jnp.bfloat16)
        den_send[h] = acc[ROWS:, HD:].T[0:8, :]
        num_copy(h).start()
        den_copy(h).start()

        @pl.when(h >= 2)
        def _():
            finish(h - 2)

        return 0

    lax.fori_loop(0, KVH, one_head, 0)
    finish(KVH - 2)
    finish(KVH - 1)

    load_wo.wait()

    def wait_att(h, _):
        for off in range(1, 8):
            att_copy(h, off).wait_recv()
        att_local(h).wait()
        return 0

    lax.fori_loop(0, EARLY, wait_att, 0)
    arrived = jnp.concatenate([att_recv[h].reshape(SLOTS, HD) for h in range(EARLY)], axis=1)

    def project_early(n, _):
        out_acc[n] = jnp.dot(
            arrived,
            wo[0 : EARLY * HD, pl.ds(pl.multiple_of(n * NW, NW), NW)],
            preferred_element_type=jnp.float32,
        )
        return 0

    lax.fori_loop(0, NC, project_early, 0)
    lax.fori_loop(EARLY, KVH, wait_att, 0)

    def exp_copy(n, off):
        r = peer(off)
        return remote(
            exp_send.at[n, r],
            exp_recv.at[n, expert],
            exp_s.at[n, off],
            exp_r.at[n, off],
            at_expert(r),
        )

    def exp_local(n):
        return pltpu.make_async_copy(
            exp_send.at[n, expert], exp_recv.at[n, expert], local_sem.at[16 + n]
        )

    late = jnp.concatenate([att_recv[h].reshape(SLOTS, HD) for h in range(EARLY, KVH)], axis=1)

    def project_out(n, _):
        part = out_acc[n] + jnp.dot(
            late,
            wo[EARLY * HD :, pl.ds(pl.multiple_of(n * NW, NW), NW)],
            preferred_element_type=jnp.float32,
        )
        exp_send[n] = part.astype(jnp.bfloat16).reshape(EXPERTS, CAP, NW)
        for off in range(1, 8):
            exp_copy(n, off).start()
        exp_local(n).start()
        return 0

    lax.fori_loop(0, NC, project_out, 0)

    def combine(n, _):
        for off in range(1, 8):
            exp_copy(n, off).wait_recv()
        exp_local(n).wait()
        back = exp_recv[n].reshape(SLOTS, NW)
        columns = pl.ds(pl.multiple_of(n * NW, NW), NW)
        mixed = jnp.dot(gates[:, 0:SLOTS], back, preferred_element_type=jnp.float32)
        mixed += jnp.dot(gates[:, SLOTS:], back, preferred_element_type=jnp.float32)
        out[:, columns] = (tokens[:, columns].astype(jnp.float32) + mixed).astype(jnp.bfloat16)
        return 0

    lax.fori_loop(0, NC, combine, 0)

    def drain_rows(k, _):
        for off in range(1, 8):
            rows_copy(k, off).wait_send()
            exp_copy(k, off).wait_send()
        return 0

    lax.fori_loop(0, KC, drain_rows, 0)

    def drain_heads(h, _):
        for way in range(3):
            kv_own_copy(h, way).wait_send()
        for way in range(2):
            kv_forward(h, way).wait_send()
        for which in range(4):
            kv_share(h, which).wait_send()
        qx_copy(h).wait_send()
        num_copy(h).wait_send()
        den_copy(h).wait_send()
        for off in range(1, 8):
            att_copy(h, off).wait_send()
        return 0

    lax.fori_loop(0, KVH, drain_heads, 0)
    for off in range(1, 8):
        bias_copy(off).wait_send()
        for p in range(PAIRS):
            q_copy(p, off).wait_send()


def layer(*operands):
    bf = jnp.bfloat16
    f32 = jnp.float32
    anywhere = pl.BlockSpec(memory_space=pl.ANY)
    inside = pl.BlockSpec(memory_space=pltpu.VMEM)
    scalars = pl.BlockSpec(memory_space=pltpu.SMEM)
    dma = pltpu.SemaphoreType.DMA
    return pl.pallas_call(
        kernel,
        out_shape=jax.ShapeDtypeStruct((NEW_DEV, D), bf),
        in_specs=[scalars] * 3 + [inside] * 7 + [anywhere] * 6,
        out_specs=inside,
        scratch_shapes=[
            pltpu.VMEM((KVH, 2 * NZ, KEYS, 2 * HD), bf),
            pltpu.VMEM((2 * NZ, 8, BIAS_WIDTH), f32),
            pltpu.VMEM((KC, EXPERTS, CAP, KW), bf),
            pltpu.VMEM((D, KVW), bf),
            pltpu.VMEM((KVW, D), bf),
            pltpu.VMEM((SLOTS, KVW), f32),
            pltpu.VMEM((PAIRS, EXPERTS, CAP, PAIR), bf),
            pltpu.VMEM((PAIRS, EXPERTS, CAP, PAIR), bf),
            pltpu.VMEM((KVH, 2 * ROWS, HD), bf),
            pltpu.VMEM((2 * ROWS, 2 * HD), f32),
            pltpu.VMEM((KVH, ROWS, 2 * HD), f32),
            pltpu.VMEM((KVH, ROWS, HD), bf),
            pltpu.VMEM((KVH, ROWS, HD), bf),
            pltpu.VMEM((KVH, 8, ROWS), f32),
            pltpu.VMEM((KVH, 8, ROWS), f32),
            pltpu.VMEM((KVH, EXPERTS, CAP, HD), bf),
            pltpu.VMEM((KVH, EXPERTS, CAP, HD), bf),
            pltpu.VMEM((NC, EXPERTS, CAP, NW), bf),
            pltpu.VMEM((NC, EXPERTS, CAP, NW), bf),
            pltpu.VMEM((NC, SLOTS, NW), f32),
            pltpu.VMEM((PAIRS, D, PAIR), bf),
            pltpu.VMEM((PAIRS, D, PAIR), bf),
            pltpu.VMEM((CACHE_DEV, KVW), bf),
            pltpu.VMEM((CACHE_DEV, KVW), bf),
            pltpu.VMEM((NEW_DEV + CB, D), bf),
            pltpu.VMEM((KC, EXPERTS, CAP, KW), bf),
            pltpu.VMEM((8, BIAS_WIDTH), f32),
            pltpu.VMEM((ROWS, SLOTS), bf),
            pltpu.VMEM((SLOTS, ROWS), bf),
            pltpu.VMEM((NEW_DEV, 2 * SLOTS), bf),
            pltpu.VMEM((NEW_DEV + CB, HD), f32),
            pltpu.VMEM((NEW_DEV + CB, HD), f32),
            dma((40,)),
            dma((KC, 8)),
            dma((KC, 8)),
            dma((PAIRS, 8)),
            dma((PAIRS, 8)),
            dma((KVH, 9)),
            dma((KVH, 9)),
            dma((8,)),
            dma((8,)),
            dma((KVH,)),
            dma((KVH,)),
            dma((KVH,)),
            dma((KVH,)),
            dma((KVH,)),
            dma((KVH,)),
            dma((KVH, 8)),
            dma((KVH, 8)),
            dma((NC, 8)),
            dma((NC, 8)),
        ],
        compiler_params=pltpu.CompilerParams(
            collective_id=0, has_side_effects=True, vmem_limit_bytes=63 * 1024 * 1024
        ),
        name="layer",
    )(*operands)


def shards(
    new_tokens,
    norm_gain,
    router_weight,
    att_choice,
    w_query,
    w_key,
    w_value,
    w_out,
    cache_keys,
    cache_values,
    hidden_held,
    recompute_ids,
    block_live,
    cached_len,
):
    blk_index = lax.axis_index("blk")
    frequency = jnp.exp(
        (jnp.arange(HD, dtype=jnp.int32) % (HD // 2)).astype(jnp.float32)
        * (-math.log(theta_base) / (HD // 2))
    )
    new_base = (cached_len[0] + blk_index * NEW_DEV).astype(jnp.float32) * frequency
    held_base = (blk_index * CACHE_DEV + recompute_ids[0, 0] * CB).astype(jnp.float32) * frequency
    angles = jnp.stack([new_base, new_base, held_base, held_base])
    odd = jnp.arange(4)[:, None] % 2 == 1
    base = jnp.where(odd, jnp.sin(angles), jnp.cos(angles))
    wave = np.exp((np.arange(HD) % (HD // 2)) * (-math.log(theta_base) / (HD // 2)))
    turns = np.arange(NEW_DEV)[:, None] * wave[None, :]
    step = jnp.asarray(np.stack([np.cos(turns), np.sin(turns)]), jnp.float32)
    mixed = layer(
        cached_len,
        recompute_ids,
        block_live,
        new_tokens[0],
        hidden_held[0],
        norm_gain[None, :],
        att_choice[0].T,
        router_weight.T,
        base,
        step,
        w_key,
        w_value,
        cache_keys[0],
        cache_values[0],
        w_query[0],
        w_out[0],
    )
    return mixed[None]


def solution(mesh):
    placed = (
        P("expert", "blk", None),
        P(),
        P(),
        P("expert", "blk", None),
        P("expert", None, None),
        P(),
        P(),
        P("expert", None, None),
        P("expert", "blk", None),
        P("expert", "blk", None),
        P("expert", "blk", None),
        P("expert", "blk"),
        P("expert", "blk"),
        P("expert"),
    )
    return jax.shard_map(
        shards, mesh=mesh, in_specs=placed, out_specs=P("expert", "blk", None), check_vma=False
    )
```

```python
import math

import jax
import jax.numpy as jnp
import numpy as np
from jax import lax
from jax.experimental import pallas as pl
from jax.experimental.pallas import tpu as pltpu
from jax.sharding import PartitionSpec as P

HD = 128
KVH = 8
CB = 32
CAP = 64
D = 2048
KVW = KVH * HD
NEW_DEV = 128
CACHE_DEV = 320
KEYS = NEW_DEV + CACHE_DEV
HALF = KEYS // 2
EXPERTS = 8
SLOTS = EXPERTS * CAP
ROWS = 2 * NEW_DEV
KC = 4
KW = D // KC
NC = 4
NW = D // NC
NZ = 4
PAIRS = 4
PAIR = 2 * HD
BLK_DEV = 10
BIAS_WIDTH = 384
EARLY = 6
ORDER = (6, 5, 7, 4, 2, 1, 3)
PASS_AT = (3, 4, 5, 6, 7)

epsilon = 1e-06
theta_base = 10000.0
MASKED = -1e30
LOG2E = 1.4426950408889634
SCALE = LOG2E / math.sqrt(HD)


def product_nt(left, right):
    return lax.dot_general(
        left, right, (((1,), (1,)), ((), ())), preferred_element_type=jnp.float32
    )


def kernel(
    length_ref,
    held_ref,
    live_ref,
    tokens,
    hidden,
    gain,
    choice,
    router,
    base,
    step,
    w_key,
    w_value,
    cache_keys,
    cache_values,
    w_query,
    w_out,
    out,
    kv,
    bias,
    rows,
    wq,
    wo,
    qacc,
    qsend,
    qret,
    queries,
    acc,
    own_part,
    num_send,
    num_recv,
    den_send,
    den_recv,
    att_send,
    att_recv,
    exp_send,
    exp_recv,
    out_acc,
    wk,
    wv,
    old_k,
    old_v,
    both,
    rows_send,
    bias_own,
    gather_q,
    spread_q,
    gates,
    cosine,
    sine,
    local_sem,
    rows_s,
    rows_r,
    qs_s,
    qs_r,
    kv_s,
    kv_r,
    bias_s,
    bias_r,
    qx_s,
    qx_r,
    num_s,
    num_r,
    den_s,
    den_r,
    att_s,
    att_r,
    exp_s,
    exp_r,
):
    blk = lax.axis_index("blk")
    expert = lax.axis_index("expert")
    z = blk // 4
    xl = (blk // 2) % 2
    c = blk % 2
    xh = expert // 4
    y = expert % 4

    def at_blk(zz, xx, cc):
        return {"blk": zz * 4 + xx * 2 + cc, "expert": expert}

    def peer(off):
        return ((xh + off // 4) % 2) * 4 + (y + off % 4) % 4

    def at_expert(e):
        return {"blk": blk, "expert": e}

    zp = (z + 1) % NZ
    zm = (z + NZ - 1) % NZ
    zo = (z + 2) % NZ
    up = at_blk(zp, xl, c)
    down = at_blk(zm, xl, c)
    partner = at_blk(z, xl, 1 - c)
    across = at_blk(z, 1 - xl, c)
    mine = z * 2 + c

    def remote(src, dst, ssem, rsem, device):
        return pltpu.make_async_remote_copy(
            src_ref=src,
            dst_ref=dst,
            send_sem=ssem,
            recv_sem=rsem,
            device_id=device,
            device_id_type=pl.DeviceIdType.MESH,
        )

    barrier = pltpu.get_barrier_semaphore()
    for off in ORDER:
        pl.semaphore_signal(
            barrier, inc=1, device_id=at_expert(peer(off)), device_id_type=pl.DeviceIdType.MESH
        )
        pl.semaphore_signal(
            barrier,
            inc=1,
            device_id=at_blk((z + off // 2) % NZ, xl, (c + off % 2) % 2),
            device_id_type=pl.DeviceIdType.MESH,
        )
    pl.semaphore_signal(barrier, inc=1, device_id=across, device_id_type=pl.DeviceIdType.MESH)

    load_wq = pltpu.make_async_copy(w_query, wq, local_sem.at[0])
    load_wo = pltpu.make_async_copy(w_out, wo, local_sem.at[1])

    def load_wk(p):
        columns = pl.ds(p * PAIR, PAIR)
        return pltpu.make_async_copy(w_key.at[:, columns], wk.at[p], local_sem.at[20 + p])

    def load_wv(p):
        columns = pl.ds(p * PAIR, PAIR)
        return pltpu.make_async_copy(w_value.at[:, columns], wv.at[p], local_sem.at[24 + p])

    load_old_k = pltpu.make_async_copy(cache_keys, old_k, local_sem.at[28])
    load_old_v = pltpu.make_async_copy(cache_values, old_v, local_sem.at[29])
    load_old_k.start()
    load_old_v.start()
    for p in range(PAIRS):
        load_wk(p).start()
        load_wv(p).start()
    load_wq.start()
    load_wo.start()

    def norm(hidden_rows):
        widened = hidden_rows.astype(jnp.float32)
        inverse = lax.rsqrt(jnp.mean(widened * widened, axis=-1, keepdims=True) + epsilon)
        return (widened * inverse * gain[...]).astype(jnp.bfloat16)

    both[0:NEW_DEV] = norm(tokens[...])
    both[NEW_DEV:] = norm(hidden[...])

    def rows_copy(k, off):
        e = peer(off)
        return remote(
            rows_send.at[k, e],
            rows.at[k, expert],
            rows_s.at[k, off],
            rows_r.at[k, off],
            at_expert(e),
        )

    def rows_local(k):
        return pltpu.make_async_copy(
            rows_send.at[k, expert],
            rows.at[k, expert],
            local_sem.at[3 + k],
        )

    def kv_own_copy(h, way):
        return remote(
            kv.at[h, mine],
            kv.at[h, mine],
            kv_s.at[h, way],
            kv_r.at[h, way],
            (up, down, partner)[way],
        )

    def kv_forward(h, way):
        source = (zm, zp)[way] * 2 + c
        part = pl.ds(way * HALF, HALF)
        return remote(
            kv.at[h, source, part],
            kv.at[h, source, part],
            kv_s.at[h, 3 + way],
            kv_r.at[h, 3 + way],
            (up, down)[way],
        )

    def kv_share(h, which):
        if which < 2:
            ref = kv.at[h, (zm, zp)[which] * 2 + c]
        else:
            ref = kv.at[h, zo * 2 + c, pl.ds((which - 2) * HALF, HALF)]
        return remote(ref, ref, kv_s.at[h, 5 + which], kv_r.at[h, 5 + which], partner)

    def bias_copy(off):
        return remote(
            bias_own,
            bias.at[mine],
            bias_s.at[off],
            bias_r.at[off],
            at_blk((z + off // 2) % NZ, xl, (c + off % 2) % 2),
        )

    cb = base[0:1, :]
    sb = base[1:2, :]
    ch = base[2:3, :]
    sh = base[3:4, :]
    ct = step[0]
    st = step[1]
    sign = jnp.where(lax.broadcasted_iota(jnp.int32, (1, HD), 1) < HD // 2, -1.0, 1.0)
    cosine[0:NEW_DEV] = cb * ct - sb * st
    sine[0:NEW_DEV] = (sb * ct + cb * st) * sign
    cosine[NEW_DEV:] = ch * ct[0:CB] - sh * st[0:CB]
    sine[NEW_DEV:] = (sh * ct[0:CB] + ch * st[0:CB]) * sign
    place = lax.broadcasted_iota(jnp.int32, (8, BIAS_WIDTH), 1)
    live = jnp.zeros((8, BIAS_WIDTH), jnp.int32)
    for j in range(BLK_DEV):
        live = jnp.where(place // CB == j, live_ref[0, j], live)
    usable = (live == 1) & (blk * CACHE_DEV + place < length_ref[0])
    bias_own[...] = jnp.where(usable, 0.0, MASKED)
    bias[mine] = bias_own[...]

    load_old_k.wait()
    load_old_v.wait()
    held = lax.broadcasted_iota(jnp.int32, (CACHE_DEV, HD), 0) // CB == held_ref[0, 0]

    def own_pair(p):
        load_wk(p).wait()
        load_wv(p).wait()
        keys = jnp.dot(both[...], wk[p], preferred_element_type=jnp.float32)
        values = jnp.dot(both[...], wv[p], preferred_element_type=jnp.float32)
        for i in range(2):
            h = 2 * p + i
            k_head = keys[:, i * HD : (i + 1) * HD]
            k_head = k_head * cosine[...] + pltpu.roll(k_head, HD // 2, 1) * sine[...]
            v_head = values[:, i * HD : (i + 1) * HD]
            for new, old, at in ((k_head, old_k, 0), (v_head, old_v, HD)):
                new = new.astype(jnp.bfloat16)
                kv[h, mine, 0:NEW_DEV, at : at + HD] = new[0:NEW_DEV]
                kv[h, mine, NEW_DEV:, at : at + HD] = jnp.where(
                    held,
                    jnp.concatenate([new[NEW_DEV:]] * BLK_DEV, axis=0),
                    old[:, h * HD : (h + 1) * HD],
                )

    def send_pair(p):
        for i in range(2):
            for way in range(3):
                kv_own_copy(2 * p + i, way).start()

    own_pair(0)
    pl.semaphore_wait(barrier, 15)
    send_pair(0)

    lane = lax.broadcasted_iota(jnp.int32, (NEW_DEV, HD), 1)
    row = lax.broadcasted_iota(jnp.int32, (NEW_DEV, HD), 0)
    earlier = (row > lane).astype(jnp.bfloat16)
    named = [
        jnp.broadcast_to(choice[k : k + 1, :].astype(jnp.float32), (HD, NEW_DEV)).T.astype(jnp.int32)
        for k in range(2)
    ]
    hot = [named[k] == lane for k in range(2)]
    count = [
        jnp.dot(earlier, jnp.where(m, 1.0, 0.0).astype(jnp.bfloat16), preferred_element_type=jnp.float32)
        for m in hot
    ]
    total = jnp.sum(jnp.where(hot[0], 1.0, 0.0), axis=0, keepdims=True)
    count[1] = count[1] + total
    slot_lane = lax.broadcasted_iota(jnp.int32, (NEW_DEV, SLOTS), 1)
    at_slot = []
    for k in range(2):
        slot = jnp.sum(jnp.where(hot[k], count[k], 0.0), axis=1, keepdims=True)
        target = named[k][:, 0:1] * CAP + slot.astype(jnp.int32)
        at_slot.append(slot_lane == target)
    placed = [jnp.where(m, 1.0, 0.0) for m in at_slot]
    gather_q[0:NEW_DEV] = placed[0].astype(jnp.bfloat16)
    gather_q[NEW_DEV:] = placed[1].astype(jnp.bfloat16)
    spread = [m.T for m in placed]
    spread_q[:, 0:NEW_DEV] = spread[0].astype(jnp.bfloat16)
    spread_q[:, NEW_DEV:] = spread[1].astype(jnp.bfloat16)
    dispatch = (spread[0] + spread[1]).astype(jnp.bfloat16)
    for k in range(KC):
        rows_send[k] = (
            jnp.dot(
                dispatch,
                both[0:NEW_DEV, k * KW : (k + 1) * KW],
                preferred_element_type=jnp.float32,
            )
            .astype(jnp.bfloat16)
            .reshape(EXPERTS, CAP, KW)
        )

    def send_rows(k, _):
        for off in ORDER:
            rows_copy(k, off).start()
        rows_local(k).start()
        return 0

    lax.fori_loop(0, KC, send_rows, 0)

    for p in range(1, PAIRS):
        own_pair(p)
        send_pair(p)
    for off in ORDER:
        bias_copy(off).start()

    logits = product_nt(both[0:NEW_DEV], router[...])
    chosen = [
        jnp.sum(jnp.where(m[:, 0:EXPERTS], logits, 0.0), axis=1, keepdims=True) for m in hot
    ]
    gate_first = jax.nn.sigmoid(chosen[0] - chosen[1])
    both_gates = jnp.where(at_slot[0], gate_first, 0.0) + jnp.where(
        at_slot[1], 1.0 - gate_first, 0.0
    )
    gates_high = both_gates.astype(jnp.bfloat16)
    gates[:, 0:SLOTS] = gates_high
    gates[:, SLOTS:] = (both_gates - gates_high.astype(jnp.float32)).astype(jnp.bfloat16)

    def pass_on(h, _):
        for way in range(2):
            kv_own_copy(h, way).wait_recv()
            kv_forward(h, way).start()
        for way in range(2):
            kv_share(h, way).start()
        return 0

    load_wq.wait()

    def project(k, _):
        for off in ORDER:
            rows_copy(k, off).wait_recv()
        rows_local(k).wait()

        @pl.when(k > 0)
        def _():
            pass_on(k - 1, 0)

        part = jnp.dot(
            rows[k].reshape(SLOTS, KW),
            wq[pl.ds(pl.multiple_of(k * KW, KW), KW), :],
            preferred_element_type=jnp.float32,
        )

        @pl.when(k == 0)
        def _():
            qacc[...] = part

        @pl.when(k > 0)
        def _():
            qacc[...] += part

        return 0

    lax.fori_loop(0, KC, project, 0)

    def q_copy(p, off):
        r = peer(off)
        return remote(
            qsend.at[p, r], qret.at[p, expert], qs_s.at[p, off], qs_r.at[p, off], at_expert(r)
        )

    def q_local(p):
        return pltpu.make_async_copy(
            qsend.at[p, expert], qret.at[p, expert], local_sem.at[30 + p]
        )

    for p in range(PAIRS):
        qsend[p] = (
            qacc[:, p * PAIR : (p + 1) * PAIR].astype(jnp.bfloat16).reshape(EXPERTS, CAP, PAIR)
        )
        for off in ORDER:
            q_copy(p, off).start()
        q_local(p).start()

    def qx_copy(h):
        return remote(
            queries.at[h, pl.ds(0, ROWS)],
            queries.at[h, pl.ds(ROWS, ROWS)],
            qx_s.at[h],
            qx_r.at[h],
            across,
        )

    cos_q = jnp.concatenate([cosine[0:NEW_DEV]] * 2, axis=0)
    sin_q = jnp.concatenate([sine[0:NEW_DEV]] * 2, axis=0)
    for p in range(PAIRS):
        lax.fori_loop(PASS_AT[p], PASS_AT[p + 1], pass_on, 0)
        for off in ORDER:
            q_copy(p, off).wait_recv()
        q_local(p).wait()
        gathered = jnp.dot(
            gather_q[...], qret[p].reshape(SLOTS, PAIR), preferred_element_type=jnp.float32
        )
        for i in range(2):
            v = gathered[:, i * HD : (i + 1) * HD]
            turned = v * cos_q + pltpu.roll(v, HD // 2, 1) * sin_q
            queries[2 * p + i, 0:ROWS] = turned.astype(jnp.bfloat16)
        for i in range(2):
            qx_copy(2 * p + i).start()
    lax.fori_loop(PASS_AT[PAIRS], KVH, pass_on, 0)
    for off in ORDER:
        bias_copy(off).wait_recv()

    lead = (
        lax.broadcasted_iota(jnp.int32, (ROWS, NEW_DEV), 0) % NEW_DEV
        - lax.broadcasted_iota(jnp.int32, (ROWS, NEW_DEV), 1)
    )

    def half(h, cc):
        old_part = slice(NEW_DEV, KEYS)
        blocks = [zz * 2 + cc for zz in range(NZ)]
        new_keys = jnp.concatenate([kv[h, j, 0:NEW_DEV, 0:HD] for j in blocks], axis=0)
        old_keys = jnp.concatenate([kv[h, j, old_part, 0:HD] for j in blocks], axis=0)
        new_scores = product_nt(queries[h], new_keys)
        old_scores = product_nt(queries[h], old_keys)
        shut = jnp.concatenate([bias[j, 0:1, 0:CACHE_DEV] for j in blocks], axis=1)
        pieces = []
        for zz, j in enumerate(blocks):
            offset_own = jnp.clip((j - mine) * NEW_DEV, -NEW_DEV, NEW_DEV)
            offset_across = jnp.clip(2 * (zz - z) + 2 * xl - 1, -1, 1) * NEW_DEV
            fresh = jnp.exp2(new_scores[:, zz * NEW_DEV : (zz + 1) * NEW_DEV] * SCALE)
            pieces.append(
                jnp.concatenate(
                    [
                        jnp.where(lead >= offset_own, fresh[0:ROWS], 0.0),
                        jnp.where(lead >= offset_across, fresh[ROWS:], 0.0),
                    ],
                    axis=0,
                ).astype(jnp.bfloat16)
            )
        pieces.append(jnp.exp2(old_scores * SCALE + shut).astype(jnp.bfloat16))
        values = jnp.concatenate(
            [kv[h, j, 0:NEW_DEV, HD : 2 * HD] for j in blocks]
            + [kv[h, j, old_part, HD : 2 * HD] for j in blocks],
            axis=0,
        )
        extended = jnp.concatenate([values, jnp.ones((NZ * KEYS, HD), jnp.bfloat16)], axis=1)
        return jnp.dot(
            jnp.concatenate(pieces, axis=1), extended, preferred_element_type=jnp.float32
        )

    def num_copy(h):
        return remote(num_send.at[h], num_recv.at[h], num_s.at[h], num_r.at[h], across)

    def den_copy(h):
        return remote(den_send.at[h], den_recv.at[h], den_s.at[h], den_r.at[h], across)

    def att_copy(h, off):
        e = peer(off)
        return remote(
            att_send.at[h, e],
            att_recv.at[h, expert],
            att_s.at[h, off],
            att_r.at[h, off],
            at_expert(e),
        )

    def att_local(h):
        return pltpu.make_async_copy(
            att_send.at[h, expert], att_recv.at[h, expert], local_sem.at[8 + h]
        )

    def finish(h):
        num_copy(h).wait_recv()
        den_copy(h).wait_recv()
        den_there = jnp.broadcast_to(den_recv[h][0:1, :], (HD, ROWS)).T
        numerator = own_part[h, :, 0:HD] + num_recv[h].astype(jnp.float32)
        denominator = own_part[h, :, HD:] + den_there
        attended = (numerator / denominator).astype(jnp.bfloat16)
        spread = jnp.dot(spread_q[...], attended, preferred_element_type=jnp.float32)
        att_send[h] = spread.astype(jnp.bfloat16).reshape(EXPERTS, CAP, HD)
        for off in ORDER:
            att_copy(h, off).start()
        att_local(h).start()

    def one_head(h, _):
        for way in range(2):
            kv_forward(h, way).wait_recv()
            kv_share(h, 2 + way).start()
        qx_copy(h).wait_recv()

        def side(i, _):
            @pl.when(i == 1)
            def _():
                kv_own_copy(h, 2).wait_recv()
                for which in range(4):
                    kv_share(h, which).wait_recv()

            part = half(h, (c + i) % 2)

            @pl.when(i == 0)
            def _():
                acc[...] = part

            @pl.when(i == 1)
            def _():
                acc[...] += part

            return 0

        lax.fori_loop(0, 2, side, 0)
        own_part[h] = acc[0:ROWS]
        num_send[h] = acc[ROWS:, 0:HD].astype(jnp.bfloat16)
        den_send[h] = acc[ROWS:, HD:].T[0:8, :]
        num_copy(h).start()
        den_copy(h).start()

        @pl.when(h >= 2)
        def _():
            finish(h - 2)

        return 0

    lax.fori_loop(0, KVH, one_head, 0)
    finish(KVH - 2)
    finish(KVH - 1)

    load_wo.wait()

    def wait_att(h, _):
        for off in ORDER:
            att_copy(h, off).wait_recv()
        att_local(h).wait()
        return 0

    lax.fori_loop(0, EARLY, wait_att, 0)
    arrived = jnp.concatenate([att_recv[h].reshape(SLOTS, HD) for h in range(EARLY)], axis=1)

    def project_early(n, _):
        out_acc[n] = jnp.dot(
            arrived,
            wo[0 : EARLY * HD, pl.ds(pl.multiple_of(n * NW, NW), NW)],
            preferred_element_type=jnp.float32,
        )
        return 0

    lax.fori_loop(0, NC, project_early, 0)
    lax.fori_loop(EARLY, KVH, wait_att, 0)

    def exp_copy(n, off):
        r = peer(off)
        return remote(
            exp_send.at[n, r],
            exp_recv.at[n, expert],
            exp_s.at[n, off],
            exp_r.at[n, off],
            at_expert(r),
        )

    def exp_local(n):
        return pltpu.make_async_copy(
            exp_send.at[n, expert], exp_recv.at[n, expert], local_sem.at[16 + n]
        )

    late = jnp.concatenate([att_recv[h].reshape(SLOTS, HD) for h in range(EARLY, KVH)], axis=1)

    def project_out(n, _):
        part = out_acc[n] + jnp.dot(
            late,
            wo[EARLY * HD :, pl.ds(pl.multiple_of(n * NW, NW), NW)],
            preferred_element_type=jnp.float32,
        )
        exp_send[n] = part.astype(jnp.bfloat16).reshape(EXPERTS, CAP, NW)
        for off in ORDER:
            exp_copy(n, off).start()
        exp_local(n).start()
        return 0

    lax.fori_loop(0, NC, project_out, 0)

    def combine(n, _):
        for off in ORDER:
            exp_copy(n, off).wait_recv()
        exp_local(n).wait()
        back = exp_recv[n].reshape(SLOTS, NW)
        columns = pl.ds(pl.multiple_of(n * NW, NW), NW)
        mixed = jnp.dot(gates[:, 0:SLOTS], back, preferred_element_type=jnp.float32)
        mixed += jnp.dot(gates[:, SLOTS:], back, preferred_element_type=jnp.float32)
        out[:, columns] = (tokens[:, columns].astype(jnp.float32) + mixed).astype(jnp.bfloat16)
        return 0

    lax.fori_loop(0, NC, combine, 0)

    def drain_rows(k, _):
        for off in ORDER:
            rows_copy(k, off).wait_send()
            exp_copy(k, off).wait_send()
        return 0

    lax.fori_loop(0, KC, drain_rows, 0)

    def drain_heads(h, _):
        for way in range(3):
            kv_own_copy(h, way).wait_send()
        for way in range(2):
            kv_forward(h, way).wait_send()
        for which in range(4):
            kv_share(h, which).wait_send()
        qx_copy(h).wait_send()
        num_copy(h).wait_send()
        den_copy(h).wait_send()
        for off in ORDER:
            att_copy(h, off).wait_send()
        return 0

    lax.fori_loop(0, KVH, drain_heads, 0)
    for off in ORDER:
        bias_copy(off).wait_send()
        for p in range(PAIRS):
            q_copy(p, off).wait_send()


def layer(*operands):
    bf = jnp.bfloat16
    f32 = jnp.float32
    anywhere = pl.BlockSpec(memory_space=pl.ANY)
    inside = pl.BlockSpec(memory_space=pltpu.VMEM)
    scalars = pl.BlockSpec(memory_space=pltpu.SMEM)
    dma = pltpu.SemaphoreType.DMA
    return pl.pallas_call(
        kernel,
        out_shape=jax.ShapeDtypeStruct((NEW_DEV, D), bf),
        in_specs=[scalars] * 3 + [inside] * 7 + [anywhere] * 6,
        out_specs=inside,
        scratch_shapes=[
            pltpu.VMEM((KVH, 2 * NZ, KEYS, 2 * HD), bf),
            pltpu.VMEM((2 * NZ, 8, BIAS_WIDTH), f32),
            pltpu.VMEM((KC, EXPERTS, CAP, KW), bf),
            pltpu.VMEM((D, KVW), bf),
            pltpu.VMEM((KVW, D), bf),
            pltpu.VMEM((SLOTS, KVW), f32),
            pltpu.VMEM((PAIRS, EXPERTS, CAP, PAIR), bf),
            pltpu.VMEM((PAIRS, EXPERTS, CAP, PAIR), bf),
            pltpu.VMEM((KVH, 2 * ROWS, HD), bf),
            pltpu.VMEM((2 * ROWS, 2 * HD), f32),
            pltpu.VMEM((KVH, ROWS, 2 * HD), f32),
            pltpu.VMEM((KVH, ROWS, HD), bf),
            pltpu.VMEM((KVH, ROWS, HD), bf),
            pltpu.VMEM((KVH, 8, ROWS), f32),
            pltpu.VMEM((KVH, 8, ROWS), f32),
            pltpu.VMEM((KVH, EXPERTS, CAP, HD), bf),
            pltpu.VMEM((KVH, EXPERTS, CAP, HD), bf),
            pltpu.VMEM((NC, EXPERTS, CAP, NW), bf),
            pltpu.VMEM((NC, EXPERTS, CAP, NW), bf),
            pltpu.VMEM((NC, SLOTS, NW), f32),
            pltpu.VMEM((PAIRS, D, PAIR), bf),
            pltpu.VMEM((PAIRS, D, PAIR), bf),
            pltpu.VMEM((CACHE_DEV, KVW), bf),
            pltpu.VMEM((CACHE_DEV, KVW), bf),
            pltpu.VMEM((NEW_DEV + CB, D), bf),
            pltpu.VMEM((KC, EXPERTS, CAP, KW), bf),
            pltpu.VMEM((8, BIAS_WIDTH), f32),
            pltpu.VMEM((ROWS, SLOTS), bf),
            pltpu.VMEM((SLOTS, ROWS), bf),
            pltpu.VMEM((NEW_DEV, 2 * SLOTS), bf),
            pltpu.VMEM((NEW_DEV + CB, HD), f32),
            pltpu.VMEM((NEW_DEV + CB, HD), f32),
            dma((40,)),
            dma((KC, 8)),
            dma((KC, 8)),
            dma((PAIRS, 8)),
            dma((PAIRS, 8)),
            dma((KVH, 9)),
            dma((KVH, 9)),
            dma((8,)),
            dma((8,)),
            dma((KVH,)),
            dma((KVH,)),
            dma((KVH,)),
            dma((KVH,)),
            dma((KVH,)),
            dma((KVH,)),
            dma((KVH, 8)),
            dma((KVH, 8)),
            dma((NC, 8)),
            dma((NC, 8)),
        ],
        compiler_params=pltpu.CompilerParams(
            collective_id=0, has_side_effects=True, vmem_limit_bytes=63 * 1024 * 1024
        ),
        name="layer",
    )(*operands)


def shards(
    new_tokens,
    norm_gain,
    router_weight,
    att_choice,
    w_query,
    w_key,
    w_value,
    w_out,
    cache_keys,
    cache_values,
    hidden_held,
    recompute_ids,
    block_live,
    cached_len,
):
    blk_index = lax.axis_index("blk")
    frequency = jnp.exp(
        (jnp.arange(HD, dtype=jnp.int32) % (HD // 2)).astype(jnp.float32)
        * (-math.log(theta_base) / (HD // 2))
    )
    new_base = (cached_len[0] + blk_index * NEW_DEV).astype(jnp.float32) * frequency
    held_base = (blk_index * CACHE_DEV + recompute_ids[0, 0] * CB).astype(jnp.float32) * frequency
    angles = jnp.stack([new_base, new_base, held_base, held_base])
    odd = jnp.arange(4)[:, None] % 2 == 1
    base = jnp.where(odd, jnp.sin(angles), jnp.cos(angles))
    wave = np.exp((np.arange(HD) % (HD // 2)) * (-math.log(theta_base) / (HD // 2)))
    turns = np.arange(NEW_DEV)[:, None] * wave[None, :]
    step = jnp.asarray(np.stack([np.cos(turns), np.sin(turns)]), jnp.float32)
    mixed = layer(
        cached_len,
        recompute_ids,
        block_live,
        new_tokens[0],
        hidden_held[0],
        norm_gain[None, :],
        att_choice[0].T,
        router_weight.T,
        base,
        step,
        w_key,
        w_value,
        cache_keys[0],
        cache_values[0],
        w_query[0],
        w_out[0],
    )
    return mixed[None]


def solution(mesh):
    placed = (
        P("expert", "blk", None),
        P(),
        P(),
        P("expert", "blk", None),
        P("expert", None, None),
        P(),
        P(),
        P("expert", None, None),
        P("expert", "blk", None),
        P("expert", "blk", None),
        P("expert", "blk", None),
        P("expert", "blk"),
        P("expert", "blk"),
        P("expert"),
    )
    return jax.shard_map(
        shards, mesh=mesh, in_specs=placed, out_specs=P("expert", "blk", None), check_vma=False
    )
```

```python
import math

import jax
import jax.numpy as jnp
import numpy as np
from jax import lax
from jax.experimental import pallas as pl
from jax.experimental.pallas import tpu as pltpu
from jax.sharding import PartitionSpec as P

HD = 128
KVH = 8
CB = 32
CAP = 64
D = 2048
KVW = KVH * HD
NEW_DEV = 128
CACHE_DEV = 320
KEYS = NEW_DEV + CACHE_DEV
HALF = KEYS // 2
EXPERTS = 8
SLOTS = EXPERTS * CAP
ROWS = 2 * NEW_DEV
KC = 4
KW = D // KC
NC = 4
NW = D // NC
NZ = 4
PAIRS = 4
PAIR = 2 * HD
BLK_DEV = 10
BIAS_WIDTH = 384
EARLY = 6
ORDER = (6, 5, 7, 4, 2, 1, 3)
PASS_AT = {0: 3, 3: 4}
AHEAD = 3

epsilon = 1e-06
theta_base = 10000.0
MASKED = -1e30
LOG2E = 1.4426950408889634
SCALE = LOG2E / math.sqrt(HD)


def product_nt(left, right):
    return lax.dot_general(
        left, right, (((1,), (1,)), ((), ())), preferred_element_type=jnp.float32
    )


def kernel(
    length_ref,
    held_ref,
    live_ref,
    tokens,
    hidden,
    gain,
    choice,
    router_far,
    base,
    step_far,
    w_key,
    w_value,
    cache_keys,
    cache_values,
    w_query,
    w_out,
    out,
    kv,
    bias,
    rows,
    wq,
    wo,
    qacc,
    qsend,
    qret,
    queries,
    acc,
    own_part,
    num_send,
    num_recv,
    den_send,
    den_recv,
    att_send,
    att_recv,
    exp_send,
    exp_recv,
    out_acc,
    router,
    step,
    wk,
    wv,
    old_k,
    old_v,
    both,
    rows_send,
    bias_own,
    gather_q,
    spread_q,
    gates,
    cosine,
    sine,
    local_sem,
    rows_s,
    rows_r,
    qs_s,
    qs_r,
    kv_s,
    kv_r,
    bias_s,
    bias_r,
    qx_s,
    qx_r,
    num_s,
    num_r,
    den_s,
    den_r,
    att_s,
    att_r,
    exp_s,
    exp_r,
):
    blk = lax.axis_index("blk")
    expert = lax.axis_index("expert")
    z = blk // 4
    xl = (blk // 2) % 2
    c = blk % 2
    xh = expert // 4
    y = expert % 4

    def at_blk(zz, xx, cc):
        return {"blk": zz * 4 + xx * 2 + cc, "expert": expert}

    def peer(off):
        return ((xh + off // 4) % 2) * 4 + (y + off % 4) % 4

    def at_expert(e):
        return {"blk": blk, "expert": e}

    zp = (z + 1) % NZ
    zm = (z + NZ - 1) % NZ
    zo = (z + 2) % NZ
    up = at_blk(zp, xl, c)
    down = at_blk(zm, xl, c)
    partner = at_blk(z, xl, 1 - c)
    across = at_blk(z, 1 - xl, c)
    mine = z * 2 + c

    def remote(src, dst, ssem, rsem, device):
        return pltpu.make_async_remote_copy(
            src_ref=src,
            dst_ref=dst,
            send_sem=ssem,
            recv_sem=rsem,
            device_id=device,
            device_id_type=pl.DeviceIdType.MESH,
        )

    barrier = pltpu.get_barrier_semaphore()
    for off in ORDER:
        pl.semaphore_signal(
            barrier, inc=1, device_id=at_expert(peer(off)), device_id_type=pl.DeviceIdType.MESH
        )
        pl.semaphore_signal(
            barrier,
            inc=1,
            device_id=at_blk((z + off // 2) % NZ, xl, (c + off % 2) % 2),
            device_id_type=pl.DeviceIdType.MESH,
        )
    pl.semaphore_signal(barrier, inc=1, device_id=across, device_id_type=pl.DeviceIdType.MESH)

    load_wq = pltpu.make_async_copy(w_query, wq, local_sem.at[0])
    load_wo = pltpu.make_async_copy(w_out, wo, local_sem.at[1])

    def load_wk(p):
        columns = pl.ds(p * PAIR, PAIR)
        return pltpu.make_async_copy(w_key.at[:, columns], wk.at[p], local_sem.at[20 + p])

    def load_wv(p):
        columns = pl.ds(p * PAIR, PAIR)
        return pltpu.make_async_copy(w_value.at[:, columns], wv.at[p], local_sem.at[24 + p])

    load_old_k = pltpu.make_async_copy(cache_keys, old_k, local_sem.at[28])
    load_old_v = pltpu.make_async_copy(cache_values, old_v, local_sem.at[29])
    load_step = pltpu.make_async_copy(step_far, step, local_sem.at[34])
    load_router = pltpu.make_async_copy(router_far, router, local_sem.at[35])
    load_step.start()
    load_old_k.start()
    load_old_v.start()
    for p in range(PAIRS):
        load_wk(p).start()
        load_wv(p).start()
    load_wq.start()
    load_wo.start()
    load_router.start()

    def norm(hidden_rows):
        widened = hidden_rows.astype(jnp.float32)
        inverse = lax.rsqrt(jnp.mean(widened * widened, axis=-1, keepdims=True) + epsilon)
        return (widened * inverse * gain[...]).astype(jnp.bfloat16)

    both[0:NEW_DEV] = norm(tokens[...])
    both[NEW_DEV:] = norm(hidden[...])

    def rows_copy(k, off):
        e = peer(off)
        return remote(
            rows_send.at[k, e],
            rows.at[k, expert],
            rows_s.at[k, off],
            rows_r.at[k, off],
            at_expert(e),
        )

    def rows_local(k):
        return pltpu.make_async_copy(
            rows_send.at[k, expert],
            rows.at[k, expert],
            local_sem.at[3 + k],
        )

    def kv_own_copy(h, way):
        return remote(
            kv.at[h, mine],
            kv.at[h, mine],
            kv_s.at[h, way],
            kv_r.at[h, way],
            (up, down, partner)[way],
        )

    def kv_forward(h, way):
        source = (zm, zp)[way] * 2 + c
        part = pl.ds(way * HALF, HALF)
        return remote(
            kv.at[h, source, part],
            kv.at[h, source, part],
            kv_s.at[h, 3 + way],
            kv_r.at[h, 3 + way],
            (up, down)[way],
        )

    def kv_share(h, which):
        if which < 2:
            ref = kv.at[h, (zm, zp)[which] * 2 + c]
        else:
            ref = kv.at[h, zo * 2 + c, pl.ds((which - 2) * HALF, HALF)]
        return remote(ref, ref, kv_s.at[h, 5 + which], kv_r.at[h, 5 + which], partner)

    def bias_copy(off):
        return remote(
            bias_own,
            bias.at[mine],
            bias_s.at[off],
            bias_r.at[off],
            at_blk((z + off // 2) % NZ, xl, (c + off % 2) % 2),
        )

    cb = base[0:1, :]
    sb = base[1:2, :]
    ch = base[2:3, :]
    sh = base[3:4, :]
    load_step.wait()
    ct = step[0]
    st = step[1]
    sign = jnp.where(lax.broadcasted_iota(jnp.int32, (1, HD), 1) < HD // 2, -1.0, 1.0)
    cosine[0:NEW_DEV] = cb * ct - sb * st
    sine[0:NEW_DEV] = (sb * ct + cb * st) * sign
    cosine[NEW_DEV:] = ch * ct[0:CB] - sh * st[0:CB]
    sine[NEW_DEV:] = (sh * ct[0:CB] + ch * st[0:CB]) * sign
    place = lax.broadcasted_iota(jnp.int32, (8, BIAS_WIDTH), 1)
    live = jnp.zeros((8, BIAS_WIDTH), jnp.int32)
    for j in range(BLK_DEV):
        live = jnp.where(place // CB == j, live_ref[0, j], live)
    usable = (live == 1) & (blk * CACHE_DEV + place < length_ref[0])
    bias_own[...] = jnp.where(usable, 0.0, MASKED)
    bias[mine] = bias_own[...]

    load_old_k.wait()
    load_old_v.wait()
    held = lax.broadcasted_iota(jnp.int32, (CACHE_DEV, HD), 0) // CB == held_ref[0, 0]

    def own_pair(p):
        load_wk(p).wait()
        load_wv(p).wait()
        keys = jnp.dot(both[...], wk[p], preferred_element_type=jnp.float32)
        values = jnp.dot(both[...], wv[p], preferred_element_type=jnp.float32)
        for i in range(2):
            h = 2 * p + i
            k_head = keys[:, i * HD : (i + 1) * HD]
            k_head = k_head * cosine[...] + pltpu.roll(k_head, HD // 2, 1) * sine[...]
            v_head = values[:, i * HD : (i + 1) * HD]
            for new, old, at in ((k_head, old_k, 0), (v_head, old_v, HD)):
                new = new.astype(jnp.bfloat16)
                kv[h, mine, 0:NEW_DEV, at : at + HD] = new[0:NEW_DEV]
                kv[h, mine, NEW_DEV:, at : at + HD] = jnp.where(
                    held,
                    jnp.concatenate([new[NEW_DEV:]] * BLK_DEV, axis=0),
                    old[:, h * HD : (h + 1) * HD],
                )

    def send_pair(p):
        for h in range(2 * p, min(2 * p + 2, AHEAD)):
            for way in range(3):
                kv_own_copy(h, way).start()

    own_pair(0)
    pl.semaphore_wait(barrier, 15)
    send_pair(0)

    lane = lax.broadcasted_iota(jnp.int32, (NEW_DEV, HD), 1)
    row = lax.broadcasted_iota(jnp.int32, (NEW_DEV, HD), 0)
    earlier = (row > lane).astype(jnp.bfloat16)
    named = [
        jnp.broadcast_to(choice[k : k + 1, :].astype(jnp.float32), (HD, NEW_DEV)).T.astype(jnp.int32)
        for k in range(2)
    ]
    hot = [named[k] == lane for k in range(2)]
    count = [
        jnp.dot(earlier, jnp.where(m, 1.0, 0.0).astype(jnp.bfloat16), preferred_element_type=jnp.float32)
        for m in hot
    ]
    total = jnp.sum(jnp.where(hot[0], 1.0, 0.0), axis=0, keepdims=True)
    count[1] = count[1] + total
    slot_lane = lax.broadcasted_iota(jnp.int32, (NEW_DEV, SLOTS), 1)
    at_slot = []
    for k in range(2):
        slot = jnp.sum(jnp.where(hot[k], count[k], 0.0), axis=1, keepdims=True)
        target = named[k][:, 0:1] * CAP + slot.astype(jnp.int32)
        at_slot.append(slot_lane == target)
    placed = [jnp.where(m, 1.0, 0.0) for m in at_slot]
    gather_q[0:NEW_DEV] = placed[0].astype(jnp.bfloat16)
    gather_q[NEW_DEV:] = placed[1].astype(jnp.bfloat16)
    spread = [m.T for m in placed]
    spread_q[:, 0:NEW_DEV] = spread[0].astype(jnp.bfloat16)
    spread_q[:, NEW_DEV:] = spread[1].astype(jnp.bfloat16)
    dispatch = (spread[0] + spread[1]).astype(jnp.bfloat16)
    for k in range(KC):
        rows_send[k] = (
            jnp.dot(
                dispatch,
                both[0:NEW_DEV, k * KW : (k + 1) * KW],
                preferred_element_type=jnp.float32,
            )
            .astype(jnp.bfloat16)
            .reshape(EXPERTS, CAP, KW)
        )

    def send_rows(k, _):
        for off in ORDER:
            rows_copy(k, off).start()
        rows_local(k).start()
        return 0

    lax.fori_loop(0, KC, send_rows, 0)

    for p in range(1, PAIRS):
        own_pair(p)
        send_pair(p)
    for off in ORDER:
        bias_copy(off).start()

    load_router.wait()
    logits = product_nt(both[0:NEW_DEV], router[...])
    chosen = [
        jnp.sum(jnp.where(m[:, 0:EXPERTS], logits, 0.0), axis=1, keepdims=True) for m in hot
    ]
    gate_first = jax.nn.sigmoid(chosen[0] - chosen[1])
    both_gates = jnp.where(at_slot[0], gate_first, 0.0) + jnp.where(
        at_slot[1], 1.0 - gate_first, 0.0
    )
    gates_high = both_gates.astype(jnp.bfloat16)
    gates[:, 0:SLOTS] = gates_high
    gates[:, SLOTS:] = (both_gates - gates_high.astype(jnp.float32)).astype(jnp.bfloat16)

    def pass_on(h, more):
        for way in range(2):
            kv_own_copy(h, way).wait_recv()
            kv_forward(h, way).start()
        for way in range(2):
            kv_share(h, way).start()
        if more:
            for way in range(3):
                kv_own_copy(h + AHEAD, way).start()

    load_wq.wait()

    def project(k, _):
        for off in ORDER:
            rows_copy(k, off).wait_recv()
        rows_local(k).wait()

        @pl.when(k > 0)
        def _():
            pass_on(k - 1, True)

        part = jnp.dot(
            rows[k].reshape(SLOTS, KW),
            wq[pl.ds(pl.multiple_of(k * KW, KW), KW), :],
            preferred_element_type=jnp.float32,
        )

        @pl.when(k == 0)
        def _():
            qacc[...] = part

        @pl.when(k > 0)
        def _():
            qacc[...] += part

        return 0

    lax.fori_loop(0, KC, project, 0)

    def q_copy(p, off):
        r = peer(off)
        return remote(
            qsend.at[p, r], qret.at[p, expert], qs_s.at[p, off], qs_r.at[p, off], at_expert(r)
        )

    def q_local(p):
        return pltpu.make_async_copy(
            qsend.at[p, expert], qret.at[p, expert], local_sem.at[30 + p]
        )

    for p in range(PAIRS):
        qsend[p] = (
            qacc[:, p * PAIR : (p + 1) * PAIR].astype(jnp.bfloat16).reshape(EXPERTS, CAP, PAIR)
        )
        for off in ORDER:
            q_copy(p, off).start()
        q_local(p).start()

    def qx_copy(h):
        return remote(
            queries.at[h, pl.ds(0, ROWS)],
            queries.at[h, pl.ds(ROWS, ROWS)],
            qx_s.at[h],
            qx_r.at[h],
            across,
        )

    cos_q = jnp.concatenate([cosine[0:NEW_DEV]] * 2, axis=0)
    sin_q = jnp.concatenate([sine[0:NEW_DEV]] * 2, axis=0)
    for p in range(PAIRS):
        if p in PASS_AT:
            pass_on(PASS_AT[p], True)
        for off in ORDER:
            q_copy(p, off).wait_recv()
        q_local(p).wait()
        gathered = jnp.dot(
            gather_q[...], qret[p].reshape(SLOTS, PAIR), preferred_element_type=jnp.float32
        )
        for i in range(2):
            v = gathered[:, i * HD : (i + 1) * HD]
            turned = v * cos_q + pltpu.roll(v, HD // 2, 1) * sin_q
            queries[2 * p + i, 0:ROWS] = turned.astype(jnp.bfloat16)
        for i in range(2):
            qx_copy(2 * p + i).start()
    for off in ORDER:
        bias_copy(off).wait_recv()

    lead = (
        lax.broadcasted_iota(jnp.int32, (ROWS, NEW_DEV), 0) % NEW_DEV
        - lax.broadcasted_iota(jnp.int32, (ROWS, NEW_DEV), 1)
    )

    def half(h, cc):
        old_part = slice(NEW_DEV, KEYS)
        blocks = [zz * 2 + cc for zz in range(NZ)]
        new_keys = jnp.concatenate([kv[h, j, 0:NEW_DEV, 0:HD] for j in blocks], axis=0)
        old_keys = jnp.concatenate([kv[h, j, old_part, 0:HD] for j in blocks], axis=0)
        new_scores = product_nt(queries[h], new_keys)
        old_scores = product_nt(queries[h], old_keys)
        shut = jnp.concatenate([bias[j, 0:1, 0:CACHE_DEV] for j in blocks], axis=1)
        pieces = []
        for zz, j in enumerate(blocks):
            offset_own = jnp.clip((j - mine) * NEW_DEV, -NEW_DEV, NEW_DEV)
            offset_across = jnp.clip(2 * (zz - z) + 2 * xl - 1, -1, 1) * NEW_DEV
            fresh = jnp.exp2(new_scores[:, zz * NEW_DEV : (zz + 1) * NEW_DEV] * SCALE)
            pieces.append(
                jnp.concatenate(
                    [
                        jnp.where(lead >= offset_own, fresh[0:ROWS], 0.0),
                        jnp.where(lead >= offset_across, fresh[ROWS:], 0.0),
                    ],
                    axis=0,
                ).astype(jnp.bfloat16)
            )
        pieces.append(jnp.exp2(old_scores * SCALE + shut).astype(jnp.bfloat16))
        values = jnp.concatenate(
            [kv[h, j, 0:NEW_DEV, HD : 2 * HD] for j in blocks]
            + [kv[h, j, old_part, HD : 2 * HD] for j in blocks],
            axis=0,
        )
        extended = jnp.concatenate([values, jnp.ones((NZ * KEYS, HD), jnp.bfloat16)], axis=1)
        return jnp.dot(
            jnp.concatenate(pieces, axis=1), extended, preferred_element_type=jnp.float32
        )

    def num_copy(h):
        return remote(num_send.at[h], num_recv.at[h], num_s.at[h], num_r.at[h], across)

    def den_copy(h):
        return remote(den_send.at[h], den_recv.at[h], den_s.at[h], den_r.at[h], across)

    def att_copy(h, off):
        e = peer(off)
        return remote(
            att_send.at[h, e],
            att_recv.at[h, expert],
            att_s.at[h, off],
            att_r.at[h, off],
            at_expert(e),
        )

    def att_local(h):
        return pltpu.make_async_copy(
            att_send.at[h, expert], att_recv.at[h, expert], local_sem.at[8 + h]
        )

    def finish(h):
        num_copy(h).wait_recv()
        den_copy(h).wait_recv()
        den_there = jnp.broadcast_to(den_recv[h][0:1, :], (HD, ROWS)).T
        numerator = own_part[h, :, 0:HD] + num_recv[h].astype(jnp.float32)
        denominator = own_part[h, :, HD:] + den_there
        attended = (numerator / denominator).astype(jnp.bfloat16)
        spread = jnp.dot(spread_q[...], attended, preferred_element_type=jnp.float32)
        att_send[h] = spread.astype(jnp.bfloat16).reshape(EXPERTS, CAP, HD)
        for off in ORDER:
            att_copy(h, off).start()
        att_local(h).start()

    def one_head(h, _):
        @pl.when((h % 2 == 0) & (h < 6))
        def _():
            pass_on(5 + h // 2, False)

        for way in range(2):
            kv_forward(h, way).wait_recv()
            kv_share(h, 2 + way).start()
        qx_copy(h).wait_recv()

        def side(i, _):
            @pl.when(i == 1)
            def _():
                kv_own_copy(h, 2).wait_recv()
                for which in range(4):
                    kv_share(h, which).wait_recv()

            part = half(h, (c + i) % 2)

            @pl.when(i == 0)
            def _():
                acc[...] = part

            @pl.when(i == 1)
            def _():
                acc[...] += part

            return 0

        lax.fori_loop(0, 2, side, 0)
        own_part[h] = acc[0:ROWS]
        num_send[h] = acc[ROWS:, 0:HD].astype(jnp.bfloat16)
        den_send[h] = acc[ROWS:, HD:].T[0:8, :]
        num_copy(h).start()
        den_copy(h).start()

        @pl.when(h >= 2)
        def _():
            finish(h - 2)

        return 0

    lax.fori_loop(0, KVH, one_head, 0)
    finish(KVH - 2)
    finish(KVH - 1)

    load_wo.wait()

    def wait_att(h, _):
        for off in ORDER:
            att_copy(h, off).wait_recv()
        att_local(h).wait()
        return 0

    lax.fori_loop(0, EARLY, wait_att, 0)
    arrived = jnp.concatenate([att_recv[h].reshape(SLOTS, HD) for h in range(EARLY)], axis=1)

    def project_early(n, _):
        out_acc[n] = jnp.dot(
            arrived,
            wo[0 : EARLY * HD, pl.ds(pl.multiple_of(n * NW, NW), NW)],
            preferred_element_type=jnp.float32,
        )
        return 0

    lax.fori_loop(0, NC, project_early, 0)
    lax.fori_loop(EARLY, KVH, wait_att, 0)

    def exp_copy(n, off):
        r = peer(off)
        return remote(
            exp_send.at[n, r],
            exp_recv.at[n, expert],
            exp_s.at[n, off],
            exp_r.at[n, off],
            at_expert(r),
        )

    def exp_local(n):
        return pltpu.make_async_copy(
            exp_send.at[n, expert], exp_recv.at[n, expert], local_sem.at[16 + n]
        )

    late = jnp.concatenate([att_recv[h].reshape(SLOTS, HD) for h in range(EARLY, KVH)], axis=1)

    def project_out(n, _):
        part = out_acc[n] + jnp.dot(
            late,
            wo[EARLY * HD :, pl.ds(pl.multiple_of(n * NW, NW), NW)],
            preferred_element_type=jnp.float32,
        )
        exp_send[n] = part.astype(jnp.bfloat16).reshape(EXPERTS, CAP, NW)
        for off in ORDER:
            exp_copy(n, off).start()
        exp_local(n).start()
        return 0

    lax.fori_loop(0, NC, project_out, 0)

    def combine(n, _):
        for off in ORDER:
            exp_copy(n, off).wait_recv()
        exp_local(n).wait()
        back = exp_recv[n].reshape(SLOTS, NW)
        columns = pl.ds(pl.multiple_of(n * NW, NW), NW)
        mixed = jnp.dot(gates[:, 0:SLOTS], back, preferred_element_type=jnp.float32)
        mixed += jnp.dot(gates[:, SLOTS:], back, preferred_element_type=jnp.float32)
        out[:, columns] = (tokens[:, columns].astype(jnp.float32) + mixed).astype(jnp.bfloat16)
        return 0

    lax.fori_loop(0, NC, combine, 0)

    def drain_rows(k, _):
        for off in ORDER:
            rows_copy(k, off).wait_send()
            exp_copy(k, off).wait_send()
        return 0

    lax.fori_loop(0, KC, drain_rows, 0)

    def drain_heads(h, _):
        for way in range(3):
            kv_own_copy(h, way).wait_send()
        for way in range(2):
            kv_forward(h, way).wait_send()
        for which in range(4):
            kv_share(h, which).wait_send()
        qx_copy(h).wait_send()
        num_copy(h).wait_send()
        den_copy(h).wait_send()
        for off in ORDER:
            att_copy(h, off).wait_send()
        return 0

    lax.fori_loop(0, KVH, drain_heads, 0)
    for off in ORDER:
        bias_copy(off).wait_send()
        for p in range(PAIRS):
            q_copy(p, off).wait_send()


def layer(*operands):
    bf = jnp.bfloat16
    f32 = jnp.float32
    anywhere = pl.BlockSpec(memory_space=pl.ANY)
    inside = pl.BlockSpec(memory_space=pltpu.VMEM)
    scalars = pl.BlockSpec(memory_space=pltpu.SMEM)
    dma = pltpu.SemaphoreType.DMA
    return pl.pallas_call(
        kernel,
        out_shape=jax.ShapeDtypeStruct((NEW_DEV, D), bf),
        in_specs=[scalars] * 3 + [inside] * 4 + [anywhere, inside] + [anywhere] * 7,
        out_specs=inside,
        scratch_shapes=[
            pltpu.VMEM((KVH, 2 * NZ, KEYS, 2 * HD), bf),
            pltpu.VMEM((2 * NZ, 8, BIAS_WIDTH), f32),
            pltpu.VMEM((KC, EXPERTS, CAP, KW), bf),
            pltpu.VMEM((D, KVW), bf),
            pltpu.VMEM((KVW, D), bf),
            pltpu.VMEM((SLOTS, KVW), f32),
            pltpu.VMEM((PAIRS, EXPERTS, CAP, PAIR), bf),
            pltpu.VMEM((PAIRS, EXPERTS, CAP, PAIR), bf),
            pltpu.VMEM((KVH, 2 * ROWS, HD), bf),
            pltpu.VMEM((2 * ROWS, 2 * HD), f32),
            pltpu.VMEM((KVH, ROWS, 2 * HD), f32),
            pltpu.VMEM((KVH, ROWS, HD), bf),
            pltpu.VMEM((KVH, ROWS, HD), bf),
            pltpu.VMEM((KVH, 8, ROWS), f32),
            pltpu.VMEM((KVH, 8, ROWS), f32),
            pltpu.VMEM((KVH, EXPERTS, CAP, HD), bf),
            pltpu.VMEM((KVH, EXPERTS, CAP, HD), bf),
            pltpu.VMEM((NC, EXPERTS, CAP, NW), bf),
            pltpu.VMEM((NC, EXPERTS, CAP, NW), bf),
            pltpu.VMEM((NC, SLOTS, NW), f32),
            pltpu.VMEM((EXPERTS, D), bf),
            pltpu.VMEM((2, NEW_DEV, HD), f32),
            pltpu.VMEM((PAIRS, D, PAIR), bf),
            pltpu.VMEM((PAIRS, D, PAIR), bf),
            pltpu.VMEM((CACHE_DEV, KVW), bf),
            pltpu.VMEM((CACHE_DEV, KVW), bf),
            pltpu.VMEM((NEW_DEV + CB, D), bf),
            pltpu.VMEM((KC, EXPERTS, CAP, KW), bf),
            pltpu.VMEM((8, BIAS_WIDTH), f32),
            pltpu.VMEM((ROWS, SLOTS), bf),
            pltpu.VMEM((SLOTS, ROWS), bf),
            pltpu.VMEM((NEW_DEV, 2 * SLOTS), bf),
            pltpu.VMEM((NEW_DEV + CB, HD), f32),
            pltpu.VMEM((NEW_DEV + CB, HD), f32),
            dma((40,)),
            dma((KC, 8)),
            dma((KC, 8)),
            dma((PAIRS, 8)),
            dma((PAIRS, 8)),
            dma((KVH, 9)),
            dma((KVH, 9)),
            dma((8,)),
            dma((8,)),
            dma((KVH,)),
            dma((KVH,)),
            dma((KVH,)),
            dma((KVH,)),
            dma((KVH,)),
            dma((KVH,)),
            dma((KVH, 8)),
            dma((KVH, 8)),
            dma((NC, 8)),
            dma((NC, 8)),
        ],
        compiler_params=pltpu.CompilerParams(
            collective_id=0, has_side_effects=True, vmem_limit_bytes=63 * 1024 * 1024
        ),
        name="layer",
    )(*operands)


def shards(
    new_tokens,
    norm_gain,
    router_weight,
    att_choice,
    w_query,
    w_key,
    w_value,
    w_out,
    cache_keys,
    cache_values,
    hidden_held,
    recompute_ids,
    block_live,
    cached_len,
):
    blk_index = lax.axis_index("blk")
    frequency = jnp.exp(
        (jnp.arange(HD, dtype=jnp.int32) % (HD // 2)).astype(jnp.float32)
        * (-math.log(theta_base) / (HD // 2))
    )
    new_base = (cached_len[0] + blk_index * NEW_DEV).astype(jnp.float32) * frequency
    held_base = (blk_index * CACHE_DEV + recompute_ids[0, 0] * CB).astype(jnp.float32) * frequency
    angles = jnp.stack([new_base, new_base, held_base, held_base])
    odd = jnp.arange(4)[:, None] % 2 == 1
    base = jnp.where(odd, jnp.sin(angles), jnp.cos(angles))
    wave = np.exp((np.arange(HD) % (HD // 2)) * (-math.log(theta_base) / (HD // 2)))
    turns = np.arange(NEW_DEV)[:, None] * wave[None, :]
    step = jnp.asarray(np.stack([np.cos(turns), np.sin(turns)]), jnp.float32)
    mixed = layer(
        cached_len,
        recompute_ids,
        block_live,
        new_tokens[0],
        hidden_held[0],
        norm_gain[None, :],
        att_choice[0].T,
        router_weight.T,
        base,
        step,
        w_key,
        w_value,
        cache_keys[0],
        cache_values[0],
        w_query[0],
        w_out[0],
    )
    return mixed[None]


def solution(mesh):
    placed = (
        P("expert", "blk", None),
        P(),
        P(),
        P("expert", "blk", None),
        P("expert", None, None),
        P(),
        P(),
        P("expert", None, None),
        P("expert", "blk", None),
        P("expert", "blk", None),
        P("expert", "blk", None),
        P("expert", "blk"),
        P("expert", "blk"),
        P("expert"),
    )
    return jax.shard_map(
        shards, mesh=mesh, in_specs=placed, out_specs=P("expert", "blk", None), check_vma=False
    )
```
